256 devices in a mesh: seq: 32 (over z, y), head: 8 (over x, core).
Axes of the slice: x: 4, y: 4, z: 8, core: 2. Of those that a mesh axis runs over, the one named last changes fastest.
Arguments:
- x_heads: bfloat16 [4096, 131072], P(('head', 'seq')), may hold values from -6 to 6
- b_proj: bfloat16 [131072, 128], P(('seq', 'head')), may hold values from -0.5 to 0.5
- c_proj: bfloat16 [131072, 128], P(('seq', 'head')), may hold values from -6 to 6
- log_gate: float32 [64, 131072], P('head', 'seq'), may hold values from -3 to 0, as said below
- step_size: float32 [64, 131072], P('head', 'seq'), may hold values from 0.003 to 0.03
- level_weight: float32 [64, 10, 131072], P('head', None, 'seq'), may hold values from 0.25 to 4
- skip: float32 [64], P('head'), may hold values from 0.5 to 1.5
Outputs:
- y_heads: bfloat16 [4096, 131072], P(('head', 'seq'))
The draws below stay inside these ranges and needn't reach their ends.
Inputs may be any that keep to these rules, and one draw needn't show every extreme that they name: log_gate holds no positive values.
All inputs are finite; a program needn't handle non-finite values.
Results may differ from the reference program's by a relative error of at most 0.0064.
Values may be sent and summed in bfloat16 or wider, within the bound.
A program may use at most 192 MiB of HBM per device.

```python
import math
import jax
import jax.numpy as jnp
import numpy as np
from jax import lax

H = 64
P_SIZE = 64
N = 128
Q = 256
TOKEN_COUNT = 131072
LEVELS = 10


def draw_log_gate(key, part):
    sequence_lanes = jax.random.split(key, 6)
    fast_share = 0.5
    is_fast = jax.random.uniform(sequence_lanes[0], (H,)) < fast_share
    fast_rate = jax.random.uniform(sequence_lanes[1], (H,), minval=1.0 / 50.0, maxval=1.0 / 30.0)
    slow_rate = jax.random.uniform(sequence_lanes[2], (H,), minval=0.2, maxval=0.8) / TOKEN_COUNT
    head_decay_rate = jnp.where(is_fast, fast_rate, slow_rate)
    random_noise = jnp.exp(jax.random.uniform(sequence_lanes[3], (H, TOKEN_COUNT), minval=-math.log(2.0), maxval=math.log(2.0)))
    surge_position = jax.random.randint(sequence_lanes[4], (3,), 0, TOKEN_COUNT)
    surge_log_value = jax.random.uniform(sequence_lanes[5], (3,), minval=math.log(0.5), maxval=math.log(0.8))
    token_positions = jnp.arange(TOKEN_COUNT)
    surge_events = jnp.sum(jnp.where(token_positions[None, :] == surge_position[:, None], surge_log_value[:, None], 0.0), axis=0)
    return (-head_decay_rate[:, None] * random_noise + surge_events[None, :]).astype(jnp.float32)


def levels(stream_key, shape, pieces, smallest, high):
    loudness, own = 1.0, jax.random.fold_in(stream_key, 6)
    for position, blocks in pieces:
        steps = jnp.exp(jax.random.uniform(jax.random.fold_in(own, position), (blocks,), jnp.float32, smallest / len(pieces), high / len(pieces)))
        loudness = loudness * jnp.repeat(steps, shape[position] // blocks).reshape([-1 if axis == position else 1 for axis in range(len(shape))])
    return loudness


def noise(rng, dims, width, most, pieces=(), held_as=jnp.bfloat16):
    level = levels(rng, dims, pieces, -0.22, 0.18) if pieces else 1.0
    result = jax.random.normal(rng, dims, jnp.float32) * width * level
    return jnp.minimum(jnp.maximum(result, -most), most).astype(held_as)


def setup_inputs(seed: int = 0) -> dict:
    splits = jax.random.split(jax.random.key(seed), 8)
    return {
        "x_heads": noise(splits[0], (H * P_SIZE, TOKEN_COUNT), 1.0, 6.0, ((0, 256),)),
        "b_proj": noise(splits[1], (TOKEN_COUNT, N), N ** -0.5, 0.5, ((0, 256),)),
        "c_proj": noise(splits[2], (TOKEN_COUNT, N), 1.0, 6.0, ((0, 256),)),
        "log_gate": draw_log_gate(jax.random.fold_in(splits[7], 71), 0),
        "step_size": jnp.clip(jnp.exp(math.log(0.03) - 2.3025851 * jax.random.uniform(splits[4], (H, TOKEN_COUNT), jnp.float32) ** levels(splits[4], (H, TOKEN_COUNT), ((0, 8), (1, 32)), -0.2, 0.2)), 0.003, 0.03),
        "level_weight": jnp.clip(jnp.exp(math.log(4.0) - 2.7725887 * jax.random.uniform(splits[5], (H, LEVELS, TOKEN_COUNT), jnp.float32) ** levels(splits[5], (H, LEVELS, TOKEN_COUNT), ((0, 8), (2, 32)), -0.2, 0.2)), 0.25, 4.0),
        "skip": jnp.clip(0.5 + 1.0 * jax.random.uniform(splits[6], (H,), jnp.float32) ** levels(splits[6], (H,), ((0, 8),), -0.2, 0.2), 0.5, 1.5),
    }


very_negative = -1.0e30


def head_output(head_values, gate_row, step_row, weight_rows, skip_one, query_all, key_all, scores):
    span_total = TOKEN_COUNT // Q
    tree_levels = LEVELS - 1
    cumulative = jnp.cumsum(gate_row.reshape(span_total, Q), axis=1)
    step_blocks = step_row.reshape(span_total, Q)
    token_positions = jnp.arange(Q)
    causal = token_positions[:, None] >= token_positions[None, :]
    log_gaps = jnp.where(causal[None], cumulative[:, :, None] - cumulative[:, None, :], very_negative)
    mixing = (scores * jnp.exp(log_gaps) * step_blocks[:, None, :]).astype(jnp.bfloat16)
    values = head_values.reshape(P_SIZE, span_total, Q).astype(jnp.float32)
    local_part = jnp.einsum('cij,pcj->pci', mixing.astype(jnp.float32), values)
    local_part = local_part * weight_rows[0].reshape(span_total, Q)[None]
    span_log = cumulative[:, -1]
    weighted = (values * (jnp.exp(span_log[:, None] - cumulative) * step_blocks)[None]).astype(jnp.bfloat16)
    states = jnp.einsum('cjn,pcj->cnp', key_all, weighted.astype(jnp.float32))
    starts = jnp.concatenate([jnp.zeros((1,), jnp.float32), jnp.cumsum(span_log)])
    aggregate = states
    block_log = span_log
    level_part = jnp.zeros((P_SIZE, span_total, Q), jnp.float32)
    span_ids = np.arange(span_total)
    for depth_bit in range(tree_levels):
        blocks = span_ids >> depth_bit
        left_block = np.maximum(blocks - 1, 0)
        has_bit = ((blocks & 1) == 1).astype(np.float32)
        decays = jnp.exp(starts[span_ids] - starts[blocks << depth_bit]) * has_bit
        level_state = (aggregate[left_block] * decays[:, None, None]).astype(jnp.bfloat16)
        scaled = (weight_rows[depth_bit + 1].reshape(span_total, Q)[:, :, None] * query_all).astype(jnp.bfloat16)
        level_part = level_part + jnp.einsum('cin,cnp->pci', scaled.astype(jnp.float32), level_state.astype(jnp.float32))
        if depth_bit + 1 < tree_levels:
            pairs = aggregate.reshape(-1, 2, N, P_SIZE)
            pair_logs = block_log.reshape(-1, 2)
            aggregate = jnp.exp(pair_logs[:, 1])[:, None, None] * pairs[:, 0] + pairs[:, 1]
            block_log = pair_logs[:, 0] + pair_logs[:, 1]
    output_tile = local_part + jnp.exp(cumulative)[None] * level_part + skip_one * values
    return output_tile.reshape(P_SIZE, TOKEN_COUNT).astype(jnp.bfloat16)


def reference(x_heads, b_proj, c_proj, log_gate, step_size, level_weight, skip):
    span_total = TOKEN_COUNT // Q
    key_all = b_proj.astype(jnp.float32).reshape(span_total, Q, N)
    query_all = c_proj.astype(jnp.float32).reshape(span_total, Q, N)
    scores = jnp.einsum('cin,cjn->cij', query_all, key_all)
    head_rows = x_heads.reshape(H, P_SIZE, TOKEN_COUNT)

    def one_head(packed):
        head_values, gate_row, step_row, weight_rows, skip_one = packed
        return head_output(head_values, gate_row, step_row, weight_rows, skip_one, query_all, key_all, scores)

    outputs = lax.map(one_head, (head_rows, log_gate, step_size, level_weight, skip))
    return outputs.reshape(H * P_SIZE, TOKEN_COUNT)
```

```python
import functools

import jax
import jax.numpy as jnp
import numpy as np
from jax import lax
from jax.experimental import pallas as pl
from jax.experimental.pallas import tpu as pltpu
from jax.sharding import Mesh, PartitionSpec as P

P_SIZE = 64
N = 128
Q = 256
LO = 4
SPANS = 1 << LO
SHARD = SPANS * Q
LOG2E = 1.4426950408889634
NT = (((1,), (1,)), ((), ()))
F32 = jnp.float32
BF16 = jnp.bfloat16


def dot(a, b):
    return jnp.dot(a, b, preferred_element_type=F32)


def dot_nt(a, b):
    return lax.dot_general(a, b, NT, preferred_element_type=F32)


def span_cols(k):
    return pl.ds(pl.multiple_of(k * Q, Q), Q)


def states_body(lev, x_ref, b_ref, gp_ref, slow_ref, rows_ref, sum_ref, tot_ref, g_scr, st_scr):
    for k in range(SPANS):
        piece = gp_ref[0, lev : lev + 6, k * Q : (k + 1) * Q].astype(F32)
        for m in range(3):
            g_scr[m, k : k + 1, :] = piece[m : m + 1]
        g_scr[3, k : k + 1, :] = piece[3:4] + piece[4:5] + piece[5:6]
    upper = (
        lax.broadcasted_iota(jnp.int32, (Q, Q), 0) <= lax.broadcasted_iota(jnp.int32, (Q, Q), 1)
    ).astype(BF16)
    cum = dot(g_scr[0].astype(BF16), upper)
    cum = cum + dot(g_scr[1].astype(BF16), upper)
    cum = (cum + dot(g_scr[2].astype(BF16), upper)) * LOG2E
    step = g_scr[3]
    decay = jnp.exp2(cum[:, Q - 1 :] - cum) * step
    g_scr[0] = decay
    for k in range(SPANS):
        rows_ref[0, k, 0:1, :] = cum[k : k + 1]
        rows_ref[0, k, 1:2, :] = step[k : k + 1]
    logs = [jnp.broadcast_to(cum[k : k + 1, Q - 1 :], (1, N)) for k in range(SPANS)]
    starts = [jnp.zeros((1, N), F32)]
    for k in range(SPANS):
        starts.append(starts[-1] + logs[k])
    for k in range(SPANS):
        rows_ref[0, k, 2:3, :] = jnp.concatenate([starts[k], starts[k]], axis=1)

    def one(k, carry):
        cols = span_cols(k)
        w = x_ref[:, cols].astype(F32) * g_scr[0, pl.ds(k, 1), :]
        st_scr[k] = dot(w.astype(BF16), b_ref[pl.ds(pl.multiple_of(k * Q, Q), Q), :])
        return carry

    lax.fori_loop(0, SPANS, one, 0)
    agg = [st_scr[k] for k in range(SPANS)]
    block_logs = list(logs)
    for bit in range(LO):
        for k in range(SPANS):
            if (k >> bit) & 1:
                left = agg[(k >> bit) - 1]
                scale = jnp.exp2(starts[k] - starts[(k >> bit) << bit])
                slow_ref[0, k, bit * P_SIZE : (bit + 1) * P_SIZE, :] = (left * scale).astype(BF16)
            else:
                slow_ref[0, k, bit * P_SIZE : (bit + 1) * P_SIZE, :] = jnp.zeros((P_SIZE, N), BF16)
        agg = [
            jnp.exp2(block_logs[2 * m + 1]) * agg[2 * m] + agg[2 * m + 1]
            for m in range(len(agg) // 2)
        ]
        block_logs = [block_logs[2 * m] + block_logs[2 * m + 1] for m in range(len(block_logs) // 2)]
    sum_ref[0] = agg[0]
    tot_ref[0] = jnp.broadcast_to(block_logs[0], (8, N))


def main_body(lev, x_ref, b_ref, c_ref, gp_ref, slow_ref, shi_ref, rows_ref, skip_ref, out_ref):
    hi = lev - 1 - LO
    half = Q // 2
    tri = lax.broadcasted_iota(jnp.int32, (half, half), 0) <= lax.broadcasted_iota(
        jnp.int32, (half, half), 1
    )
    skip = skip_ref[0:1, 0:1]

    def one(k, carry):
        cols = span_cols(k)
        toks = pl.ds(pl.multiple_of(k * Q, Q), Q)
        x = x_ref[:, cols].astype(F32)
        b = b_ref[toks, :]
        c = c_ref[toks, :]
        tile = rows_ref[0, k]
        cum = tile[0:1, :]
        cum_col = jnp.transpose(tile)[:, 0:1]
        xs = (x * tile[1:2, :]).astype(BF16)
        top = dot_nt(b[:half], c) * jnp.exp2(cum - cum_col[:half])
        low = dot_nt(b[half:], c[half:]) * jnp.exp2(cum[:, half:] - cum_col[half:])
        m00 = jnp.where(tri, top[:, :half], 0.0).astype(BF16)
        m01 = top[:, half:].astype(BF16)
        m11 = jnp.where(tri, low, 0.0).astype(BF16)
        left = dot(xs[:, :half], m00)
        right = dot(xs, jnp.concatenate([m01, m11], axis=0))
        local = jnp.concatenate([left, right], axis=1)
        lw = gp_ref[0, :, cols].astype(F32)
        r_lo = dot_nt(slow_ref[0, k], c)
        r_hi = dot_nt(shi_ref[0], c)
        e_lo = jnp.exp2(cum)
        e_hi = jnp.exp2(cum + tile[2:3, :])
        acc = local * lw[0:1] + skip * x
        for bit in range(LO):
            acc = acc + r_lo[bit * P_SIZE : (bit + 1) * P_SIZE] * (lw[1 + bit : 2 + bit] * e_lo)
        for bit in range(hi):
            at = 1 + LO + bit
            acc = acc + r_hi[bit * P_SIZE : (bit + 1) * P_SIZE] * (lw[at : at + 1] * e_hi)
        out_ref[:, cols] = acc.astype(BF16)
        return carry

    lax.fori_loop(0, SPANS, one, 0)


def pieces(v):
    first = lax.reduce_precision(v, 8, 7)
    rest = v - first
    second = lax.reduce_precision(rest, 8, 7)
    return [first, second, rest - second]


def on_device(x_heads, b_proj, c_proj, log_gate, step_size, level_weight, skip):
    nz = lax.axis_size("z")
    ny = lax.axis_size("y")
    y_at = lax.axis_index("y")
    z_at = lax.axis_index("z")
    rows = x_heads.shape[0]
    lev = level_weight.shape[1]
    hi = lev - 1 - LO
    tok = nz * SHARD

    parts = [level_weight[:, i] for i in range(lev)] + pieces(log_gate) + pieces(step_size)
    parts += [jnp.zeros_like(log_gate)] * (16 - len(parts))
    packed = jnp.stack(parts, axis=1).astype(BF16)
    gates = lax.all_to_all(packed, "z", split_axis=0, concat_axis=0, tiled=True)
    x = x_heads.reshape(rows, nz, ny, SHARD)
    x = lax.all_to_all(x, "y", split_axis=2, concat_axis=0, tiled=True).reshape(ny * rows, tok)
    b = lax.all_gather(b_proj, ("z", "x", "core"), axis=0, tiled=True)
    c = lax.all_gather(c_proj, ("z", "x", "core"), axis=0, tiled=True)
    my_skip = jnp.broadcast_to(lax.dynamic_slice(skip, (z_at,), (1,))[:, None], (8, 128))

    x_spec = pl.BlockSpec((P_SIZE, SHARD), lambda i: (0, i))
    t_spec = pl.BlockSpec((SHARD, N), lambda i: (i, 0))
    g_spec = pl.BlockSpec((1, 16, SHARD), lambda i: (i, 0, 0))
    slow_spec = pl.BlockSpec((1, SPANS, LO * P_SIZE, N), lambda i: (i, 0, 0, 0))
    rows_spec = pl.BlockSpec((1, SPANS, 8, Q), lambda i: (i, 0, 0, 0))
    params = pltpu.CompilerParams(vmem_limit_bytes=48 << 20)
    slow, tiles, summary, total = pl.pallas_call(
        functools.partial(states_body, lev),
        grid=(nz,),
        in_specs=[x_spec, t_spec, g_spec],
        out_specs=[
            slow_spec,
            rows_spec,
            pl.BlockSpec((1, P_SIZE, N), lambda i: (i, 0, 0)),
            pl.BlockSpec((1, 8, N), lambda i: (i, 0, 0)),
        ],
        out_shape=[
            jax.ShapeDtypeStruct((nz, SPANS, LO * P_SIZE, N), BF16),
            jax.ShapeDtypeStruct((nz, SPANS, 8, Q), F32),
            jax.ShapeDtypeStruct((nz, P_SIZE, N), F32),
            jax.ShapeDtypeStruct((nz, 8, N), F32),
        ],
        scratch_shapes=[pltpu.VMEM((4, SPANS, Q), F32), pltpu.VMEM((SPANS, P_SIZE, N), F32)],
        compiler_params=params,
        name="states",
    )(x, b, gates)

    every = lax.all_gather(summary, "y", axis=1)
    logs = lax.all_gather(total[:, 0, 0], "y", axis=1).reshape(nz * ny)
    ends = jnp.cumsum(logs)
    ids = jnp.arange(nz * ny)
    mine = jnp.arange(nz) * ny + y_at
    start = jnp.sum(jnp.where(ids[None] == mine[:, None], (ends - logs)[None], 0.0), axis=1)
    bits = jnp.arange(hi)
    own = mine[:, None] >> bits[None]
    inside = (ids[None, None] >> bits[None, :, None] == own[:, :, None] - 1) & (
        (own & 1) == 1
    )[:, :, None]
    gap = jnp.where(inside, start[:, None, None] - ends[None, None], 0.0)
    weights = jnp.where(inside, jnp.exp2(gap), 0.0)
    shi = jnp.einsum(
        "zks,spn->zkpn",
        weights,
        every.reshape(nz * ny, P_SIZE, N),
        precision=lax.Precision.HIGHEST,
    )
    shi = shi.astype(BF16).reshape(nz, hi * P_SIZE, N)

    out = pl.pallas_call(
        functools.partial(main_body, lev),
        grid=(nz,),
        in_specs=[
            x_spec,
            t_spec,
            t_spec,
            g_spec,
            slow_spec,
            pl.BlockSpec((1, hi * P_SIZE, N), lambda i: (i, 0, 0)),
            rows_spec,
            pl.BlockSpec((8, 128), lambda i: (0, 0)),
        ],
        out_specs=x_spec,
        out_shape=jax.ShapeDtypeStruct((P_SIZE, tok), BF16),
        compiler_params=params,
        name="outputs",
    )(x, b, c, gates, slow, shi, tiles, my_skip)

    out = out.reshape(ny * rows, nz, 1, SHARD)
    out = lax.all_to_all(out, "y", split_axis=0, concat_axis=2, tiled=True)
    return out.reshape(rows, nz * ny * SHARD)


def build(mesh):
    group = ("x", "core")
    seq = ("z", "y")
    in_specs = (
        P(group + seq, None),
        P(seq + group, None),
        P(seq + group, None),
        P(group, seq),
        P(group, seq),
        P(group, None, seq),
        P(group),
    )
    return jax.shard_map(
        on_device, mesh=mesh, in_specs=in_specs, out_specs=P(group + seq, None), check_vma=False
    )


def solution(mesh):
    shape = (8, 4, 4, 2)
    return build(Mesh(mesh.devices.reshape(shape), ("z", "y", "x", "core")))
```

```python
import functools

import jax
import jax.numpy as jnp
from jax import lax
from jax.experimental import pallas as pl
from jax.experimental.pallas import tpu as pltpu
from jax.sharding import Mesh, PartitionSpec as P

P_SIZE = 64
N = 128
Q = 256
LO = 4
SPANS = 1 << LO
SHARD = SPANS * Q
LOG2E = 1.4426950408889634
NT = (((1,), (1,)), ((), ()))
F32 = jnp.float32
BF16 = jnp.bfloat16
MESH = pl.DeviceIdType.MESH
AXES = ("z", "y", "x", "core")


def dot(a, b):
    return jnp.dot(a, b, preferred_element_type=F32)


def dot_nt(a, b):
    return lax.dot_general(a, b, NT, preferred_element_type=F32)


def span_at(k):
    return pl.ds(pl.multiple_of(k * Q, Q), Q)


def pack_gates(lev, h, lw_ref, lg_ref, st_ref, tmp, pk):
    tmp[0:lev, :] = lw_ref[h]
    for row, ref in ((lev, lg_ref), (lev + 3, st_ref)):
        v = ref[pl.ds(h, 1), :]
        first = v.astype(BF16).astype(F32)
        rest = v - first
        second = rest.astype(BF16).astype(F32)
        tmp[row : row + 1, :] = first
        tmp[row + 1 : row + 2, :] = second
        tmp[row + 2 : row + 3, :] = rest - second
    pk[h] = tmp[...].astype(BF16)


def shard_states(lev, r, xb, bb, gb, slow, tiles, g_scr, st_scr):
    for k in range(SPANS):
        piece = gb[r, :, k * Q : (k + 1) * Q].astype(F32)
        for m in range(3):
            g_scr[m, k : k + 1, :] = piece[lev + m : lev + m + 1]
        g_scr[3, k : k + 1, :] = (
            piece[lev + 3 : lev + 4] + piece[lev + 4 : lev + 5] + piece[lev + 5 : lev + 6]
        )
    upper = (
        lax.broadcasted_iota(jnp.int32, (Q, Q), 0) <= lax.broadcasted_iota(jnp.int32, (Q, Q), 1)
    ).astype(BF16)
    cum = dot(g_scr[0].astype(BF16), upper)
    cum = cum + dot(g_scr[1].astype(BF16), upper)
    cum = (cum + dot(g_scr[2].astype(BF16), upper)) * LOG2E
    step = g_scr[3]
    g_scr[0] = jnp.exp2(cum[:, Q - 1 :] - cum) * step
    logs = [jnp.broadcast_to(cum[k : k + 1, Q - 1 :], (1, N)) for k in range(SPANS)]
    starts = [jnp.zeros((1, N), F32)]
    for k in range(SPANS):
        starts.append(starts[-1] + logs[k])
    for k in range(SPANS):
        tiles[r, k, 0:1, :] = cum[k : k + 1]
        tiles[r, k, 1:2, :] = step[k : k + 1]
        tiles[r, k, 2:3, :] = jnp.concatenate([starts[k], starts[k]], axis=1)

    def one(k, carry):
        w = xb[r, :, span_at(k)].astype(F32) * g_scr[0, pl.ds(k, 1), :]
        st_scr[k] = dot(w.astype(BF16), bb[r, span_at(k), :])
        return carry

    lax.fori_loop(0, SPANS, one, 0, unroll=2)
    agg = [st_scr[k] for k in range(SPANS)]
    block_logs = list(logs)
    for bit in range(LO):
        rows = slice(bit * P_SIZE, (bit + 1) * P_SIZE)
        for k in range(SPANS):
            if (k >> bit) & 1:
                scale = jnp.exp2(starts[k] - starts[(k >> bit) << bit])
                slow[r, k, rows, :] = (agg[(k >> bit) - 1] * scale).astype(BF16)
            else:
                slow[r, k, rows, :] = jnp.zeros((P_SIZE, N), BF16)
        pairs = range(len(agg) // 2)
        agg = [jnp.exp2(block_logs[2 * m + 1]) * agg[2 * m] + agg[2 * m + 1] for m in pairs]
        block_logs = [block_logs[2 * m] + block_logs[2 * m + 1] for m in pairs]
    return agg[0], block_logs[0]


def shard_levels(nz, ny, z, y, sums, shi):
    ybits = ny.bit_length() - 1
    zbits = nz.bit_length() - 1
    slots = [lax.rem(zz - z + nz, nz) for zz in range(nz)]
    before = [jnp.where(yy < y, 1.0, 0.0) for yy in range(ny)]
    belongs = []
    for b in range(ybits):
        own = y // (1 << b)
        odd = lax.rem(own, 2) == 1
        belongs.append(
            [jnp.where(odd & (own - 1 == yy >> b), 1.0, 0.0) for yy in range(ny)]
        )
    agg, totals, lead = [], [], []
    for zz in range(nz):
        logs = [sums[yy, slots[zz], P_SIZE : P_SIZE + 1, :] for yy in range(ny)]
        ahead = logs[0] * before[0]
        for yy in range(1, ny):
            ahead = ahead + logs[yy] * before[yy]
        lead.append(ahead)
        after = jnp.zeros((1, N), F32)
        near = jnp.zeros((1, N), F32)
        whole = None
        parts = [None] * ybits
        for yy in reversed(range(ny)):
            state = sums[yy, slots[zz], 0:P_SIZE, :]
            term = state * jnp.exp2(after)
            whole = term if whole is None else whole + term
            scale = jnp.exp2(near)
            for b in range(ybits):
                term = state * (scale * belongs[b][yy])
                parts[b] = term if parts[b] is None else parts[b] + term
            after = after + logs[yy]
            near = near + logs[yy] * before[yy]
        agg.append(whole)
        totals.append(after)
        for b in range(ybits):
            shi[slots[zz], b * P_SIZE : (b + 1) * P_SIZE, :] = parts[b].astype(BF16)
    starts = [jnp.zeros((1, N), F32)]
    for zz in range(nz):
        starts.append(starts[-1] + totals[zz])
    block_logs = list(totals)
    for b in range(zbits):
        rows = slice((ybits + b) * P_SIZE, (ybits + b + 1) * P_SIZE)
        for zz in range(nz):
            if (zz >> b) & 1:
                scale = jnp.exp2(starts[zz] - starts[(zz >> b) << b] + lead[zz])
                shi[slots[zz], rows, :] = (agg[(zz >> b) - 1] * scale).astype(BF16)
            else:
                shi[slots[zz], rows, :] = jnp.zeros((P_SIZE, N), BF16)
        pairs = range(len(agg) // 2)
        agg = [jnp.exp2(block_logs[2 * m + 1]) * agg[2 * m] + agg[2 * m + 1] for m in pairs]
        block_logs = [block_logs[2 * m] + block_logs[2 * m + 1] for m in pairs]


def shard_outputs(lev, r, skip, xb, bb, cb, gb, slow, tiles, shi, ob):
    hi = lev - 1 - LO
    half = Q // 2
    tri = lax.broadcasted_iota(jnp.int32, (half, half), 0) <= lax.broadcasted_iota(
        jnp.int32, (half, half), 1
    )

    def one(k, carry):
        at = span_at(k)
        x = xb[r, :, at].astype(F32)
        b = bb[r, at, :]
        c = cb[r, at, :]
        tile = tiles[r, k]
        cum = tile[0:1, :]
        cum_col = jnp.transpose(tile)[:, 0:1]
        xs = (x * tile[1:2, :]).astype(BF16)
        top = dot_nt(b[:half], c) * jnp.exp2(cum - cum_col[:half])
        low = dot_nt(b[half:], c[half:]) * jnp.exp2(cum[:, half:] - cum_col[half:])
        m00 = jnp.where(tri, top[:, :half], 0.0).astype(BF16)
        m01 = top[:, half:].astype(BF16)
        m11 = jnp.where(tri, low, 0.0).astype(BF16)
        left = dot(xs[:, :half], m00)
        right = dot(xs, jnp.concatenate([m01, m11], axis=0))
        local = jnp.concatenate([left, right], axis=1)
        lw = gb[r, :, at].astype(F32)
        r_lo = dot_nt(slow[r, k], c)
        r_hi = dot_nt(shi[r], c)
        e_lo = jnp.exp2(cum)
        e_hi = jnp.exp2(cum + tile[2:3, :])
        acc = local * lw[0:1] + skip * x
        for bit in range(LO):
            acc = acc + r_lo[bit * P_SIZE : (bit + 1) * P_SIZE] * (lw[1 + bit : 2 + bit] * e_lo)
        for bit in range(hi):
            row = 1 + LO + bit
            acc = acc + r_hi[bit * P_SIZE : (bit + 1) * P_SIZE] * (lw[row : row + 1] * e_hi)
        ob[r, :, at] = acc.astype(BF16)
        return carry

    lax.fori_loop(0, SPANS, one, 0, unroll=2)


def kernel(
    lev, sizes,
    x_ref, b_ref, c_ref, lg_ref, st_ref, lw_ref, skip_ref, out_ref,
    xb, bb, cb, gb, slow, tiles, sums, shi, ob, g_scr, st_scr, tmp, pk,
    l_own, l_x, l_o, s_x, r_x, s_g, r_g, s_z, r_z, s_n, r_n, s_f, r_f, s_s, r_s,
    s_m, r_m, s_o, r_o,
):
    nz, ny, nx, nc = sizes
    z, y, x, core = (lax.axis_index(a) for a in AXES)
    unit = SHARD // (nx * nc)
    rows = P_SIZE // ny
    other = 1 - core

    def turn(v, n):
        return lax.rem(v + n, n)

    def dev(dz=0, dy=0, dx=0, dc=0):
        return (turn(z + dz, nz), turn(y + dy, ny), turn(x + dx, nx), lax.rem(core + dc, nc))

    def rc(src, dst, send, recv, where):
        return pltpu.make_async_remote_copy(
            src_ref=src, dst_ref=dst, send_sem=send, recv_sem=recv,
            device_id=where, device_id_type=MESH,
        )

    def rel(i):
        odd = lax.rem(i, 2)
        return odd * ((i + 1) // 2) + (1 - odd) * lax.rem(nz - i // 2, nz)

    def cols(r, yy):
        at = (turn(z + r, nz) * ny + yy) * SHARD
        return pl.ds(pl.multiple_of(at, SHARD), SHARD)

    def band(yy):
        return pl.ds(pl.multiple_of(yy * rows, rows), rows)

    peers = [dev(dz=d) for d in range(1, nz)] + [dev(dy=d) for d in range(1, ny)]
    if nx > 1:
        peers += [dev(dx=1), dev(dx=-1)]
    if nc > 1:
        peers += [dev(dc=1)]
    barrier = pltpu.get_barrier_semaphore()
    for where in peers:
        pl.semaphore_signal(barrier, inc=1, device_id=where, device_id_type=MESH)

    src = (b_ref, c_ref)
    buf = (bb, cb)

    def piece(q, r, xx, cc, part=None):
        at = (xx * nc + cc) * unit
        size = unit
        if part is not None:
            size = unit // 2
            at = at + part * size
        return buf[q].at[r, pl.ds(pl.multiple_of(at, size), size), :]

    def own_copy(q):
        return pltpu.make_async_copy(src[q], piece(q, 0, x, core), l_own.at[q])

    def x_local(r):
        return pltpu.make_async_copy(x_ref.at[:, cols(r, y)], xb.at[r, band(y), :], l_x.at[r])

    def x_send(r, d):
        to = turn(y + d, ny)
        return rc(
            x_ref.at[:, cols(r, to)], xb.at[r, band(y), :],
            s_x.at[r, d - 1], r_x.at[r, d - 1], dev(dy=d),
        )

    def x_recv(r, d):
        to = turn(y + d, ny)
        return rc(
            x_ref.at[:, cols(r, to)], xb.at[r, band(turn(y - d, ny)), :],
            s_x.at[r, d - 1], r_x.at[r, d - 1], dev(dy=d),
        )

    def z_send(q, r):
        o = nz - r
        return rc(src[q], piece(q, r, x, core), s_z.at[q, r], r_z.at[q, r], dev(dz=o))

    def g_send(r):
        o = nz - r
        return rc(pk.at[turn(z + o, nz)], gb.at[r], s_g.at[r], r_g.at[r], dev(dz=o))

    def n_send(q, r, side, origin):
        part = piece(q, r, origin, core)
        return rc(part, part, s_n.at[q, side, r], r_n.at[q, side, r], dev(dx=1 - 2 * side))

    def f_send(q, r, side, origin):
        part = piece(q, r, origin, core, side)
        return rc(part, part, s_f.at[q, side, r], r_f.at[q, side, r], dev(dx=1 - 2 * side))

    def s_send(q, r, kind, cc):
        xx, part = ((0, None), (-1, None), (1, None), (-2, 0), (2, 1))[kind]
        ref = piece(q, r, turn(x + xx, nx), cc, part)
        return rc(ref, ref, s_s.at[q, kind, r], r_s.at[q, kind, r], dev(dc=1))

    kinds = 5 if nx > 1 else 1

    def step_a(q, i):
        r = rel(i)

        @pl.when(i == 0)
        def _():
            own_copy(q).wait()

        @pl.when(i > 0)
        def _():
            z_send(q, r).wait_recv()

        if nx > 1:
            n_send(q, r, 0, x).start()
            n_send(q, r, 1, x).start()
        if nc > 1:
            s_send(q, r, 0, core).start()

    def step_b(q, i):
        if nx > 1:
            r = rel(i)
            left, right = turn(x - 1, nx), turn(x + 1, nx)
            n_send(q, r, 0, left).wait_recv()
            f_send(q, r, 0, left).start()
            if nc > 1:
                s_send(q, r, 1, core).start()
            n_send(q, r, 1, right).wait_recv()
            f_send(q, r, 1, right).start()
            if nc > 1:
                s_send(q, r, 2, core).start()

    def step_c(q, i):
        if nx > 1:
            r = rel(i)
            far = turn(x + 2, nx)
            f_send(q, r, 0, far).wait_recv()
            if nc > 1:
                s_send(q, r, 3, core).start()
            f_send(q, r, 1, far).wait_recv()
            if nc > 1:
                s_send(q, r, 4, core).start()

    def step_s(q, i):
        if nc > 1:
            r = rel(i)
            for kind in range(kinds):
                s_send(q, r, kind, other).wait_recv()

    def m_send(r, d, yy):
        ref = sums.at[yy, r]
        return rc(ref, ref, s_m.at[r, d - 1], r_m.at[r, d - 1], dev(dy=d))

    def o_send(r, d):
        to = turn(y + d, ny)
        return rc(
            ob.at[r, band(to), :], out_ref.at[:, cols(r, y)],
            s_o.at[r, d - 1], r_o.at[r, d - 1], dev(dy=d),
        )

    def o_recv(r, d):
        to = turn(y + d, ny)
        return rc(
            ob.at[r, band(to), :], out_ref.at[:, cols(r, turn(y - d, ny))],
            s_o.at[r, d - 1], r_o.at[r, d - 1], dev(dy=d),
        )

    def o_local(r):
        return pltpu.make_async_copy(ob.at[r, band(y), :], out_ref.at[:, cols(r, y)], l_o.at[r])

    own_copy(0).start()
    own_copy(1).start()
    pack_gates(lev, z, lw_ref, lg_ref, st_ref, tmp, pk)
    gb[0] = pk[z]
    pl.semaphore_wait(barrier, len(peers))

    def begin(i, carry):
        r = rel(i)

        @pl.when(i > 0)
        def _():
            z_send(0, r).start()
            pack_gates(lev, turn(z - r, nz), lw_ref, lg_ref, st_ref, tmp, pk)
            g_send(r).start()

        x_local(r).start()
        for d in range(1, ny):
            x_send(r, d).start()
        return carry

    lax.fori_loop(0, nz, begin, 0)

    def inward(i, carry):
        @pl.when(i < nz)
        def _():
            step_a(0, i)

        @pl.when((i >= 1) & (i <= nz))
        def _():
            step_b(0, i - 1)

        @pl.when((i >= 2) & (i <= nz + 1))
        def _():
            step_c(0, i - 2)

        @pl.when((i >= 3) & (i <= nz + 1))
        def _():
            z_send(1, rel(i - 2)).start()

        @pl.when((i >= nz) & (i < 2 * nz))
        def _():
            step_a(1, i - nz)

        @pl.when(i >= nz + 1)
        def _():
            step_b(1, i - nz - 1)

        @pl.when(i >= nz + 2)
        def _():
            step_c(1, i - nz - 2)

        @pl.when(i >= 3)
        def _():
            r = rel(i - 3)
            step_s(0, i - 3)

            @pl.when(i > 3)
            def _():
                g_send(r).wait_recv()

            x_local(r).wait()
            for d in range(1, ny):
                x_recv(r, d).wait_recv()
            state, log = shard_states(lev, r, xb, bb, gb, slow, tiles, g_scr, st_scr)
            sums[y, r, 0:P_SIZE, :] = state
            sums[y, r, P_SIZE : P_SIZE + 8, :] = jnp.broadcast_to(log, (8, N))
            for d in range(1, ny):
                m_send(r, d, y).start()

        return carry

    lax.fori_loop(0, nz + 3, inward, 0)

    def gather(r, carry):
        for d in range(1, ny):
            m_send(r, d, turn(y - d, ny)).wait_recv()
        return carry

    lax.fori_loop(0, nz, gather, 0)
    shard_levels(nz, ny, z, y, sums, shi)
    skip = skip_ref[z]
    early = min(3, nz)

    def outward(i, carry):
        r = rel(i)

        @pl.when(i + early < nz)
        def _():
            step_a(1, i + early)

        @pl.when(i + 2 < nz)
        def _():
            step_b(1, i + 2)

        @pl.when(i + 1 < nz)
        def _():
            step_c(1, i + 1)

        step_s(1, i)
        shard_outputs(lev, r, skip, xb, bb, cb, gb, slow, tiles, shi, ob)
        o_local(r).start()
        for d in range(1, ny):
            o_send(r, d).start()
        return carry

    lax.fori_loop(0, nz, outward, 0)

    def finish(r, carry):
        @pl.when(r > 0)
        def _():
            g_send(r).wait_send()
            for q in range(2):
                z_send(q, r).wait_send()

        for q in range(2):
            if nx > 1:
                for side in range(2):
                    n_send(q, r, side, x).wait_send()
                    f_send(q, r, side, x).wait_send()
            if nc > 1:
                for kind in range(kinds):
                    s_send(q, r, kind, core).wait_send()
        for d in range(1, ny):
            x_send(r, d).wait_send()
            m_send(r, d, y).wait_send()
            o_send(r, d).wait_send()
        for d in range(1, ny):
            o_recv(r, d).wait_recv()
        o_local(r).wait()
        return carry

    lax.fori_loop(0, nz, finish, 0)


def on_device(x_heads, b_proj, c_proj, log_gate, step_size, level_weight, skip):
    nz, ny, nx, nc = sizes = tuple(lax.axis_size(a) for a in AXES)
    lev = level_weight.shape[1]
    hi = lev - 1 - LO
    rows, tok = x_heads.shape
    any_spec = pl.BlockSpec(memory_space=pl.ANY)
    vmem = pl.BlockSpec(memory_space=pltpu.VMEM)
    dma = lambda *shape: pltpu.SemaphoreType.DMA(shape)
    ys = max(ny - 1, 1)
    return pl.pallas_call(
        functools.partial(kernel, lev, sizes),
        out_shape=jax.ShapeDtypeStruct((rows, tok), BF16),
        in_specs=[any_spec, any_spec, any_spec, vmem, vmem, vmem,
                  pl.BlockSpec(memory_space=pltpu.SMEM)],
        out_specs=any_spec,
        scratch_shapes=[
            pltpu.VMEM((nz, P_SIZE, SHARD), BF16),
            pltpu.VMEM((nz, SHARD, N), BF16),
            pltpu.VMEM((nz, SHARD, N), BF16),
            pltpu.VMEM((nz, 16, SHARD), BF16),
            pltpu.VMEM((nz, SPANS, LO * P_SIZE, N), BF16),
            pltpu.VMEM((nz, SPANS, 8, Q), F32),
            pltpu.VMEM((ny, nz, P_SIZE + 8, N), F32),
            pltpu.VMEM((nz, hi * P_SIZE, N), BF16),
            pltpu.VMEM((nz, P_SIZE, SHARD), BF16),
            pltpu.VMEM((4, SPANS, Q), F32),
            pltpu.VMEM((SPANS, P_SIZE, N), F32),
            pltpu.VMEM((16, SHARD), F32),
            pltpu.VMEM((nz, 16, SHARD), BF16),
            dma(2), dma(nz), dma(nz),
            dma(nz, ys), dma(nz, ys),
            dma(nz), dma(nz),
            dma(2, nz), dma(2, nz),
            dma(2, 2, nz), dma(2, 2, nz),
            dma(2, 2, nz), dma(2, 2, nz),
            dma(2, 5, nz), dma(2, 5, nz),
            dma(nz, ys), dma(nz, ys),
            dma(nz, ys), dma(nz, ys),
        ],
        compiler_params=pltpu.CompilerParams(
            collective_id=0, has_side_effects=True, vmem_limit_bytes=56 << 20
        ),
        name="layer",
    )(x_heads, b_proj, c_proj, log_gate, step_size, level_weight, skip)


def build(mesh):
    group = ("x", "core")
    seq = ("z", "y")
    in_specs = (
        P(group + seq, None),
        P(seq + group, None),
        P(seq + group, None),
        P(group, seq),
        P(group, seq),
        P(group, None, seq),
        P(group),
    )
    return jax.shard_map(
        on_device, mesh=mesh, in_specs=in_specs, out_specs=P(group + seq, None), check_vma=False
    )


def solution(mesh):
    return build(Mesh(mesh.devices.reshape(8, 4, 4, 2), AXES))
```

```python
import functools

import jax
import jax.numpy as jnp
from jax import lax
from jax.experimental import pallas as pl
from jax.experimental.pallas import tpu as pltpu
from jax.sharding import Mesh, PartitionSpec as P

P_SIZE = 64
N = 128
Q = 256
LO = 4
SPANS = 1 << LO
SHARD = SPANS * Q
LOG2E = 1.4426950408889634
NT = (((1,), (1,)), ((), ()))
F32 = jnp.float32
BF16 = jnp.bfloat16
MESH = pl.DeviceIdType.MESH
AXES = ("z", "y", "x", "core")


def dot(a, b):
    return jnp.dot(a, b, preferred_element_type=F32)


def dot_nt(a, b):
    return lax.dot_general(a, b, NT, preferred_element_type=F32)


def span_at(k):
    return pl.ds(pl.multiple_of(k * Q, Q), Q)


def pack_gates(lev, h, lw_ref, lg_ref, st_ref, tmp, pk):
    for row in range(lev):
        tmp[row : row + 1, :] = lw_ref[row, pl.ds(h, 1), :]
    for row, ref in ((lev, lg_ref), (lev + 3, st_ref)):
        v = ref[pl.ds(h, 1), :]
        first = v.astype(BF16).astype(F32)
        rest = v - first
        second = rest.astype(BF16).astype(F32)
        tmp[row : row + 1, :] = first
        tmp[row + 1 : row + 2, :] = second
        tmp[row + 2 : row + 3, :] = rest - second
    pk[h] = tmp[...].astype(BF16)


def shard_states(lev, r, xb, bb, gb, slow, tiles, g_scr, st_scr):
    for k in range(SPANS):
        piece = gb[r, :, k * Q : (k + 1) * Q].astype(F32)
        for m in range(3):
            g_scr[m, k : k + 1, :] = piece[lev + m : lev + m + 1]
        g_scr[3, k : k + 1, :] = (
            piece[lev + 3 : lev + 4] + piece[lev + 4 : lev + 5] + piece[lev + 5 : lev + 6]
        )
    upper = (
        lax.broadcasted_iota(jnp.int32, (Q, Q), 0) <= lax.broadcasted_iota(jnp.int32, (Q, Q), 1)
    ).astype(BF16)
    cum = dot(g_scr[0].astype(BF16), upper)
    cum = cum + dot(g_scr[1].astype(BF16), upper)
    cum = (cum + dot(g_scr[2].astype(BF16), upper)) * LOG2E
    step = g_scr[3]
    g_scr[0] = jnp.exp2(cum[:, Q - 1 :] - cum) * step
    logs = [jnp.broadcast_to(cum[k : k + 1, Q - 1 :], (1, N)) for k in range(SPANS)]
    starts = [jnp.zeros((1, N), F32)]
    for k in range(SPANS):
        starts.append(starts[-1] + logs[k])
    for k in range(SPANS):
        tiles[r, k, 0:1, :] = cum[k : k + 1]
        tiles[r, k, 1:2, :] = step[k : k + 1]
        tiles[r, k, 2:3, :] = jnp.concatenate([starts[k], starts[k]], axis=1)

    def one(k, carry):
        w = xb[r, :, span_at(k)].astype(F32) * g_scr[0, pl.ds(k, 1), :]
        st_scr[k] = dot(w.astype(BF16), bb[r, span_at(k), :])
        return carry

    lax.fori_loop(0, SPANS, one, 0, unroll=2)
    agg = [st_scr[k] for k in range(SPANS)]
    block_logs = list(logs)
    for bit in range(LO):
        rows = slice(bit * P_SIZE, (bit + 1) * P_SIZE)
        for k in range(SPANS):
            if (k >> bit) & 1:
                scale = jnp.exp2(starts[k] - starts[(k >> bit) << bit])
                slow[r, k, rows, :] = (agg[(k >> bit) - 1] * scale).astype(BF16)
            else:
                slow[r, k, rows, :] = jnp.zeros((P_SIZE, N), BF16)
        pairs = range(len(agg) // 2)
        agg = [jnp.exp2(block_logs[2 * m + 1]) * agg[2 * m] + agg[2 * m + 1] for m in pairs]
        block_logs = [block_logs[2 * m] + block_logs[2 * m + 1] for m in pairs]
    return agg[0], block_logs[0]


def shard_levels(nz, ny, z, y, sums, shi):
    ybits = ny.bit_length() - 1
    zbits = nz.bit_length() - 1
    slots = [lax.rem(zz - z + nz, nz) for zz in range(nz)]
    before = [jnp.where(yy < y, 1.0, 0.0) for yy in range(ny)]
    belongs = []
    for b in range(ybits):
        own = y // (1 << b)
        odd = lax.rem(own, 2) == 1
        belongs.append(
            [jnp.where(odd & (own - 1 == yy >> b), 1.0, 0.0) for yy in range(ny)]
        )
    agg, totals, lead = [], [], []
    for zz in range(nz):
        logs = []
        for yy in range(ny):
            block = sums[yy, slots[zz], P_SIZE : P_SIZE + 16, :].astype(F32)
            logs.append(block[0:1] + block[1:2] + block[2:3])
        ahead = logs[0] * before[0]
        for yy in range(1, ny):
            ahead = ahead + logs[yy] * before[yy]
        lead.append(ahead)
        after = jnp.zeros((1, N), F32)
        near = jnp.zeros((1, N), F32)
        whole = None
        parts = [None] * ybits
        for yy in reversed(range(ny)):
            state = sums[yy, slots[zz], 0:P_SIZE, :].astype(F32)
            term = state * jnp.exp2(after)
            whole = term if whole is None else whole + term
            scale = jnp.exp2(near)
            for b in range(ybits):
                term = state * (scale * belongs[b][yy])
                parts[b] = term if parts[b] is None else parts[b] + term
            after = after + logs[yy]
            near = near + logs[yy] * before[yy]
        agg.append(whole)
        totals.append(after)
        for b in range(ybits):
            shi[slots[zz], b * P_SIZE : (b + 1) * P_SIZE, :] = parts[b].astype(BF16)
    starts = [jnp.zeros((1, N), F32)]
    for zz in range(nz):
        starts.append(starts[-1] + totals[zz])
    block_logs = list(totals)
    for b in range(zbits):
        rows = slice((ybits + b) * P_SIZE, (ybits + b + 1) * P_SIZE)
        for zz in range(nz):
            if (zz >> b) & 1:
                scale = jnp.exp2(starts[zz] - starts[(zz >> b) << b] + lead[zz])
                shi[slots[zz], rows, :] = (agg[(zz >> b) - 1] * scale).astype(BF16)
            else:
                shi[slots[zz], rows, :] = jnp.zeros((P_SIZE, N), BF16)
        pairs = range(len(agg) // 2)
        agg = [jnp.exp2(block_logs[2 * m + 1]) * agg[2 * m] + agg[2 * m + 1] for m in pairs]
        block_logs = [block_logs[2 * m] + block_logs[2 * m + 1] for m in pairs]


def span_mix(k, r, bb, cb, tiles, mix, slot):
    half = Q // 2
    tri = lax.broadcasted_iota(jnp.int32, (half, half), 0) <= lax.broadcasted_iota(
        jnp.int32, (half, half), 1
    )
    at = span_at(k)
    b = bb[r, at, :]
    c = cb[r, at, :]
    tile = tiles[r, k]
    cum = tile[0:1, :]
    cum_col = jnp.transpose(tile)[:, 0:1]
    top = dot_nt(b[:half], c) * jnp.exp2(cum - cum_col[:half])
    low = dot_nt(b[half:], c[half:]) * jnp.exp2(cum[:, half:] - cum_col[half:])
    mix[slot, :half, :half] = jnp.where(tri, top[:, :half], 0.0).astype(BF16)
    mix[slot, :half, half:] = top[:, half:].astype(BF16)
    mix[slot, half:, half:] = jnp.where(tri, low, 0.0).astype(BF16)


def span_out(lev, k, r, skip, xb, cb, gb, slow, tiles, shi, ob, mix, slot):
    hi = lev - 1 - LO
    at = span_at(k)
    x = xb[r, :, at].astype(F32)
    c = cb[r, at, :]
    tile = tiles[r, k]
    cum = tile[0:1, :]
    xs = (x * tile[1:2, :]).astype(BF16)
    lw = gb[r, :, at].astype(F32)
    acc = dot(xs, mix[slot]) * lw[0:1] + skip * x
    r_lo = dot_nt(slow[r, k], c)
    r_hi = dot_nt(shi[r], c)
    e_lo = jnp.exp2(cum)
    e_hi = jnp.exp2(cum + tile[2:3, :])
    for bit in range(LO):
        acc = acc + r_lo[bit * P_SIZE : (bit + 1) * P_SIZE] * (lw[1 + bit : 2 + bit] * e_lo)
    for bit in range(hi):
        row = 1 + LO + bit
        acc = acc + r_hi[bit * P_SIZE : (bit + 1) * P_SIZE] * (lw[row : row + 1] * e_hi)
    ob[r, :, at] = acc.astype(BF16)


def shard_outputs(lev, r, first, count, skip, xb, bb, cb, gb, slow, tiles, shi, ob, mix):
    span_mix(first, r, bb, cb, tiles, mix, 0)

    def two(m, carry):
        k = first + 2 * m
        span_out(lev, k, r, skip, xb, cb, gb, slow, tiles, shi, ob, mix, 0)
        span_mix(k + 1, r, bb, cb, tiles, mix, 1)
        span_out(lev, k + 1, r, skip, xb, cb, gb, slow, tiles, shi, ob, mix, 1)
        span_mix(jnp.minimum(k + 2, first + count - 1), r, bb, cb, tiles, mix, 0)
        return carry

    lax.fori_loop(0, count // 2, two, 0)


def kernel(
    lev, sizes,
    x_ref, b_ref, c_ref, lg_ref, st_ref, lw_ref, skip_ref, out_ref,
    xb, bb, cb, gb, slow, tiles, sums, shi, ob, g_scr, st_scr, tmp, pk, mix, lwb, rowb,
    l_own, l_o, sent, r_x, r_g, r_z, r_h, r_n, r_f, r_s, r_m, r_o,
):
    nz, ny, nx, nc = sizes
    z, y, x, core = (lax.axis_index(a) for a in AXES)
    unit = SHARD // (nx * nc)
    rows = P_SIZE // ny
    other = 1 - core

    def turn(v, n):
        return lax.rem(v + n, n)

    def dev(dz=0, dy=0, dx=0, dc=0):
        return (turn(z + dz, nz), turn(y + dy, ny), turn(x + dx, nx), lax.rem(core + dc, nc))

    def rc(src, dst, send, recv, where):
        return pltpu.make_async_remote_copy(
            src_ref=src, dst_ref=dst, send_sem=send, recv_sem=recv,
            device_id=where, device_id_type=MESH,
        )

    def rel(i):
        odd = lax.rem(i, 2)
        return odd * ((i + 1) // 2) + (1 - odd) * lax.rem(nz - i // 2, nz)

    def cols(r, yy):
        at = (turn(z + r, nz) * ny + yy) * SHARD
        return pl.ds(pl.multiple_of(at, SHARD), SHARD)

    def band(yy):
        return pl.ds(pl.multiple_of(yy * rows, rows), rows)

    peers = [dev(dz=d) for d in range(1, nz)] + [dev(dy=d) for d in range(1, ny)]
    if nx > 1:
        peers += [dev(dx=1), dev(dx=-1)]
    if nc > 1:
        peers += [dev(dc=1)]
    barrier = pltpu.get_barrier_semaphore()
    for where in peers:
        pl.semaphore_signal(barrier, inc=1, device_id=where, device_id_type=MESH)

    src = (b_ref, c_ref)
    buf = (bb, cb)

    def piece(q, r, xx, cc, part=None):
        at = (xx * nc + cc) * unit
        size = unit
        if part is not None:
            size = unit // 2
            at = at + part * size
        return buf[q].at[r, pl.ds(pl.multiple_of(at, size), size), :]

    def own_copy(q):
        return pltpu.make_async_copy(src[q], piece(q, 0, x, core), l_own.at[q])

    def x_local(r):
        return pltpu.make_async_copy(x_ref.at[:, cols(r, y)], xb.at[r, band(y), :], r_x.at[r])

    def x_send(r, d):
        to = turn(y + d, ny)
        return rc(
            x_ref.at[:, cols(r, to)], xb.at[r, band(y), :], sent.at[0], r_x.at[r], dev(dy=d)
        )

    def bulk(ref, send, recv):
        return rc(ref, ref, send, recv, peers[0])

    def some(q, count):
        if count % SHARD == 0:
            return buf[q].at[pl.ds(0, count // SHARD)]
        return buf[q].at[0, pl.ds(0, count), :]

    mid = nz // 2

    def z_send(q, r, side, part=None):
        to = lax.rem(r - 1 + nz, nz) if side == 0 else r + 1
        arrived = r_z.at[q, to] if part is None or side == 0 else r_h.at[q]
        return rc(
            piece(q, r, x, core, part), piece(q, to, x, core, part),
            sent.at[4 + q], arrived, dev(dz=1 - 2 * side),
        )

    def z_each(q, r, act):
        ahead = lax.rem(nz - r, nz)

        @pl.when(((r == 0) | (r > mid)) & (ahead + 1 < mid))
        def _():
            act(z_send(q, r, 0))

        @pl.when(((r == 0) | (r > mid)) & (ahead + 1 == mid))
        def _():
            act(z_send(q, r, 0, 0))

        @pl.when(r + 1 < mid)
        def _():
            act(z_send(q, r, 1))

        @pl.when(r + 1 == mid)
        def _():
            act(z_send(q, r, 1, 1))

    def z_wait(q, r):
        @pl.when(r != mid)
        def _():
            ref = piece(q, r, x, core)
            rc(ref, ref, sent.at[4 + q], r_z.at[q, r], dev(dz=1)).wait_recv()

        @pl.when(r == mid)
        def _():
            ref = piece(q, r, x, core, 0)
            rc(ref, ref, sent.at[4 + q], r_z.at[q, r], dev(dz=1)).wait_recv()
            ref = piece(q, r, x, core, 1)
            rc(ref, ref, sent.at[4 + q], r_h.at[q], dev(dz=-1)).wait_recv()

    def g_send(r):
        o = nz - r
        return rc(pk.at[turn(z + o, nz)], gb.at[r], sent.at[1], r_g.at[r], dev(dz=o))

    def n_send(q, r, side, origin):
        part = piece(q, r, origin, core)
        return rc(part, part, sent.at[6 + q], r_n.at[q, r], dev(dx=1 - 2 * side))

    def f_send(q, r, side, origin):
        part = piece(q, r, origin, core, side)
        return rc(part, part, sent.at[8 + q], r_f.at[q, r], dev(dx=1 - 2 * side))

    def s_send(q, r, kind, cc):
        xx, part = ((0, None), (-1, None), (1, None), (-2, 0), (2, 1))[kind]
        ref = piece(q, r, turn(x + xx, nx), cc, part)
        return rc(ref, ref, sent.at[10 + q], r_s.at[q, r], dev(dc=1))

    kinds = 5 if nx > 1 else 1

    def step_a(q, i):
        r = rel(i)

        @pl.when(i == 0)
        def _():
            own_copy(q).wait()

        @pl.when(i > 0)
        def _():
            z_wait(q, r)

        z_each(q, r, lambda copy: copy.start())

        if nx > 1:
            n_send(q, r, 0, x).start()
            n_send(q, r, 1, x).start()
        if nc > 1:
            s_send(q, r, 0, core).start()

    def step_b(q, i):
        if nx > 1:
            r = rel(i)
            bulk(some(q, 2 * unit), sent.at[6 + q], r_n.at[q, r]).wait_recv()
            for side, origin in ((0, turn(x - 1, nx)), (1, turn(x + 1, nx))):
                f_send(q, r, side, origin).start()
                if nc > 1:
                    s_send(q, r, 1 + side, core).start()

    def step_c(q, i):
        if nx > 1:
            r = rel(i)
            bulk(some(q, unit), sent.at[8 + q], r_f.at[q, r]).wait_recv()
            if nc > 1:
                for kind in (3, 4):
                    s_send(q, r, kind, core).start()

    def step_s(q, i):
        if nc > 1:
            r = rel(i)
            bulk(some(q, nx * unit), sent.at[10 + q], r_s.at[q, r]).wait_recv()

    def m_send(r, d):
        ref = sums.at[y, r]
        return rc(ref, ref, sent.at[2], r_m.at[0], dev(dy=d))

    part_size = SHARD // 2

    def out_cols(r, part, yy):
        at = (turn(z + r, nz) * ny + yy) * SHARD + part * part_size
        return pl.ds(pl.multiple_of(at, part_size), part_size)

    def here(part):
        return pl.ds(pl.multiple_of(part * part_size, part_size), part_size)

    def o_send(r, part, d):
        to = turn(y + d, ny)
        return rc(
            ob.at[r, band(to), here(part)], out_ref.at[:, out_cols(r, part, y)],
            sent.at[3], r_o.at[0], dev(dy=d),
        )

    def o_local(r, part):
        return pltpu.make_async_copy(
            ob.at[r, band(y), here(part)], out_ref.at[:, out_cols(r, part, y)], l_o.at[0]
        )

    loads = [
        pltpu.make_async_copy(lw_ref, lwb, l_own.at[2]),
        pltpu.make_async_copy(lg_ref, rowb.at[0], l_own.at[3]),
        pltpu.make_async_copy(st_ref, rowb.at[1], l_own.at[4]),
    ]
    own_copy(0).start()
    own_copy(1).start()
    for copy in loads:
        copy.start()
    mix[...] = jnp.zeros_like(mix)
    pl.semaphore_wait(barrier, len(peers))

    def begin(i, carry):
        r = rel(i)
        x_local(r).start()
        for d in range(1, ny):
            x_send(r, d).start()
        return carry

    lax.fori_loop(0, nz, begin, 0)
    step_a(0, 0)
    for copy in loads:
        copy.wait()
    pack_gates(lev, z, lwb, rowb.at[0], rowb.at[1], tmp, pk)
    gb[0] = pk[z]

    def inward(i, carry):
        @pl.when((i >= 1) & (i < nz))
        def _():
            step_a(0, i)

        @pl.when((i >= 1) & (i <= nz))
        def _():
            step_b(0, i - 1)

        @pl.when((i >= 2) & (i <= nz + 1))
        def _():
            step_c(0, i - 2)

        @pl.when((i >= 1) & (i < nz))
        def _():
            r = rel(i)
            pack_gates(lev, turn(z - r, nz), lwb, rowb.at[0], rowb.at[1], tmp, pk)
            g_send(r).start()

        @pl.when((i >= nz) & (i < 2 * nz))
        def _():
            step_a(1, i - nz)

        @pl.when(i >= nz + 1)
        def _():
            step_b(1, i - nz - 1)

        @pl.when(i >= nz + 2)
        def _():
            step_c(1, i - nz - 2)

        @pl.when(i >= 3)
        def _():
            r = rel(i - 3)
            step_s(0, i - 3)

            @pl.when(i > 3)
            def _():
                g_send(r).wait_recv()

            bulk(xb.at[r], sent.at[0], r_x.at[r]).wait_recv()
            state, log = shard_states(lev, r, xb, bb, gb, slow, tiles, g_scr, st_scr)
            sums[y, r, 0:P_SIZE, :] = state.astype(BF16)
            first = log.astype(BF16).astype(F32)
            rest = log - first
            second = rest.astype(BF16).astype(F32)
            logs = jnp.concatenate([first, second, rest - second, jnp.zeros((13, N), F32)], axis=0)
            sums[y, r, P_SIZE : P_SIZE + 16, :] = logs.astype(BF16)
            for d in range(1, ny):
                m_send(r, d).start()

        return carry

    lax.fori_loop(1, nz + 3, inward, 0)

    bulk(sums.at[pl.ds(0, ny - 1)], sent.at[2], r_m.at[0]).wait_recv()
    shard_levels(nz, ny, z, y, sums, shi)
    skip = skip_ref[z]
    early = min(3, nz)

    def outward(j, carry):
        i, part = j // 2, lax.rem(j, 2)
        r = rel(i)

        @pl.when(part == 0)
        def _():
            @pl.when(i + early < nz)
            def _():
                step_a(1, i + early)

            @pl.when(i + 2 < nz)
            def _():
                step_b(1, i + 2)

            @pl.when(i + 1 < nz)
            def _():
                step_c(1, i + 1)

            step_s(1, i)

        half = SPANS // 2
        shard_outputs(
            lev, r, part * half, half, skip, xb, bb, cb, gb, slow, tiles, shi, ob, mix
        )
        o_local(r, part).start()
        for d in range(1, ny):
            o_send(r, part, d).start()
        return carry

    lax.fori_loop(0, 2 * nz, outward, 0)

    away = nz * (ny - 1) * rows * SHARD // (P_SIZE * SHARD)
    bulk(xb.at[pl.ds(0, away)], sent.at[0], r_x.at[0]).wait_send()
    bulk(pk.at[pl.ds(0, nz - 1)], sent.at[1], r_g.at[0]).wait_send()
    bulk(sums.at[pl.ds(0, ny - 1)], sent.at[2], r_m.at[0]).wait_send()
    bulk(ob.at[pl.ds(0, away)], sent.at[3], r_o.at[0]).wait_send()
    for q in range(2):
        bulk(some(q, (nz - 1) * unit), sent.at[4 + q], r_h.at[q]).wait_send()
        if nx > 1:
            bulk(some(q, 2 * nz * unit), sent.at[6 + q], r_h.at[q]).wait_send()
            bulk(some(q, nz * unit), sent.at[8 + q], r_h.at[q]).wait_send()
        if nc > 1:
            bulk(some(q, nx * nz * unit), sent.at[10 + q], r_h.at[q]).wait_send()
    bulk(ob.at[pl.ds(0, away)], sent.at[3], r_o.at[0]).wait_recv()
    mine = ob.at[pl.ds(0, nz // ny)]
    pltpu.make_async_copy(mine, mine, l_o.at[0]).wait()


def on_device(x_heads, b_proj, c_proj, log_gate, step_size, level_weight, skip):
    nz, ny, nx, nc = sizes = tuple(lax.axis_size(a) for a in AXES)
    lev = level_weight.shape[1]
    hi = lev - 1 - LO
    rows, tok = x_heads.shape
    any_spec = pl.BlockSpec(memory_space=pl.ANY)
    dma = lambda *shape: pltpu.SemaphoreType.DMA(shape)
    return pl.pallas_call(
        functools.partial(kernel, lev, sizes),
        out_shape=jax.ShapeDtypeStruct((rows, tok), BF16),
        in_specs=[any_spec, any_spec, any_spec, any_spec, any_spec, any_spec,
                  pl.BlockSpec(memory_space=pltpu.SMEM)],
        out_specs=any_spec,
        scratch_shapes=[
            pltpu.VMEM((nz, P_SIZE, SHARD), BF16),
            pltpu.VMEM((nz, SHARD, N), BF16),
            pltpu.VMEM((nz, SHARD, N), BF16),
            pltpu.VMEM((nz, 16, SHARD), BF16),
            pltpu.VMEM((nz, SPANS, LO * P_SIZE, N), BF16),
            pltpu.VMEM((nz, SPANS, 8, Q), F32),
            pltpu.VMEM((ny, nz, P_SIZE + 16, N), BF16),
            pltpu.VMEM((nz, hi * P_SIZE, N), BF16),
            pltpu.VMEM((nz, P_SIZE, SHARD), BF16),
            pltpu.VMEM((4, SPANS, Q), F32),
            pltpu.VMEM((SPANS, P_SIZE, N), F32),
            pltpu.VMEM((16, SHARD), F32),
            pltpu.VMEM((nz, 16, SHARD), BF16),
            pltpu.VMEM((2, Q, Q), BF16),
            pltpu.VMEM((lev, nz, SHARD), F32),
            pltpu.VMEM((2, nz, SHARD), F32),
            dma(5), dma(1), dma(12),
            dma(nz), dma(nz), dma(2, nz), dma(2), dma(2, nz), dma(2, nz), dma(2, nz), dma(1), dma(1),
        ],
        compiler_params=pltpu.CompilerParams(
            collective_id=0, has_side_effects=True, vmem_limit_bytes=56 << 20
        ),
        name="layer",
    )(x_heads, b_proj, c_proj, log_gate, step_size, jnp.swapaxes(level_weight, 0, 1), skip)


def build(mesh):
    group = ("x", "core")
    seq = ("z", "y")
    in_specs = (
        P(group + seq, None),
        P(seq + group, None),
        P(seq + group, None),
        P(group, seq),
        P(group, seq),
        P(group, None, seq),
        P(group),
    )
    return jax.shard_map(
        on_device, mesh=mesh, in_specs=in_specs, out_specs=P(group + seq, None), check_vma=False
    )


def solution(mesh):
    return build(Mesh(mesh.devices.reshape(8, 4, 4, 2), AXES))
```

```python
import functools

import jax
import jax.numpy as jnp
from jax import lax
from jax.experimental import pallas as pl
from jax.experimental.pallas import tpu as pltpu
from jax.sharding import Mesh, PartitionSpec as P

P_SIZE = 64
N = 128
Q = 256
LO = 4
SPANS = 1 << LO
STATIC = 3
SHARD = SPANS * Q
LOG2E = 1.4426950408889634
NT = (((1,), (1,)), ((), ()))
F32 = jnp.float32
BF16 = jnp.bfloat16
MESH = pl.DeviceIdType.MESH
AXES = ("z", "y", "x", "core")


def dot(a, b):
    return jnp.dot(a, b, preferred_element_type=F32)


def dot_nt(a, b):
    return lax.dot_general(a, b, NT, preferred_element_type=F32)


def span_at(k):
    return pl.ds(pl.multiple_of(k * Q, Q), Q)


def pack_gates(lev, h, lw_ref, lg_ref, st_ref, tmp, pk):
    for row in range(lev):
        tmp[row : row + 1, :] = lw_ref[row, pl.ds(h, 1), :]
    for row, ref in ((lev, lg_ref), (lev + 3, st_ref)):
        v = ref[pl.ds(h, 1), :]
        first = v.astype(BF16).astype(F32)
        rest = v - first
        second = rest.astype(BF16).astype(F32)
        tmp[row : row + 1, :] = first
        tmp[row + 1 : row + 2, :] = second
        tmp[row + 2 : row + 3, :] = rest - second
    pk[h] = tmp[...].astype(BF16)


def shard_states(lev, r, xb, bb, gb, slow, tiles, g_scr, st_scr):
    for k in range(SPANS):
        piece = gb[r, :, k * Q : (k + 1) * Q].astype(F32)
        for m in range(3):
            g_scr[m, k : k + 1, :] = piece[lev + m : lev + m + 1]
        g_scr[3, k : k + 1, :] = (
            piece[lev + 3 : lev + 4] + piece[lev + 4 : lev + 5] + piece[lev + 5 : lev + 6]
        )
    upper = (
        lax.broadcasted_iota(jnp.int32, (Q, Q), 0) <= lax.broadcasted_iota(jnp.int32, (Q, Q), 1)
    ).astype(BF16)
    cum = dot(g_scr[0].astype(BF16), upper)
    cum = cum + dot(g_scr[1].astype(BF16), upper)
    cum = (cum + dot(g_scr[2].astype(BF16), upper)) * LOG2E
    step = g_scr[3]
    g_scr[0] = jnp.exp2(cum[:, Q - 1 :] - cum) * step
    logs = [jnp.broadcast_to(cum[k : k + 1, Q - 1 :], (1, N)) for k in range(SPANS)]
    starts = [jnp.zeros((1, N), F32)]
    for k in range(SPANS):
        starts.append(starts[-1] + logs[k])
    for k in range(SPANS):
        tiles[r, k, 0:1, :] = cum[k : k + 1]
        tiles[r, k, 1:2, :] = step[k : k + 1]
        tiles[r, k, 2:3, :] = jnp.concatenate([starts[k], starts[k]], axis=1)

    def one(k, carry):
        w = xb[r, :, span_at(k)].astype(F32) * g_scr[0, pl.ds(k, 1), :]
        st_scr[k] = dot(w.astype(BF16), bb[r, span_at(k), :])
        return carry

    lax.fori_loop(0, SPANS, one, 0, unroll=2)
    agg = [st_scr[k] for k in range(SPANS)]
    block_logs = list(logs)
    for bit in range(LO):
        rows = slice(bit * P_SIZE, (bit + 1) * P_SIZE)
        for k in range(SPANS):
            if (k >> bit) & 1:
                scale = jnp.exp2(starts[k] - starts[(k >> bit) << bit])
                slow[r, k, rows, :] = (agg[(k >> bit) - 1] * scale).astype(BF16)
            else:
                slow[r, k, rows, :] = jnp.zeros((P_SIZE, N), BF16)
        pairs = range(len(agg) // 2)
        agg = [jnp.exp2(block_logs[2 * m + 1]) * agg[2 * m] + agg[2 * m + 1] for m in pairs]
        block_logs = [block_logs[2 * m] + block_logs[2 * m + 1] for m in pairs]
    return agg[0], block_logs[0]


def shard_levels(nz, ny, z, y, sums, shi):
    ybits = ny.bit_length() - 1
    zbits = nz.bit_length() - 1
    slots = [lax.rem(zz - z + nz, nz) for zz in range(nz)]
    before = [jnp.where(yy < y, 1.0, 0.0) for yy in range(ny)]
    belongs = []
    for b in range(ybits):
        own = y // (1 << b)
        odd = lax.rem(own, 2) == 1
        belongs.append(
            [jnp.where(odd & (own - 1 == yy >> b), 1.0, 0.0) for yy in range(ny)]
        )
    agg, totals, lead = [], [], []
    for zz in range(nz):
        logs = []
        for yy in range(ny):
            block = sums[yy, slots[zz], P_SIZE : P_SIZE + 16, :].astype(F32)
            logs.append(block[0:1] + block[1:2] + block[2:3])
        ahead = logs[0] * before[0]
        for yy in range(1, ny):
            ahead = ahead + logs[yy] * before[yy]
        lead.append(ahead)
        after = jnp.zeros((1, N), F32)
        near = jnp.zeros((1, N), F32)
        whole = None
        parts = [None] * ybits
        for yy in reversed(range(ny)):
            state = sums[yy, slots[zz], 0:P_SIZE, :].astype(F32)
            term = state * jnp.exp2(after)
            whole = term if whole is None else whole + term
            scale = jnp.exp2(near)
            for b in range(ybits):
                term = state * (scale * belongs[b][yy])
                parts[b] = term if parts[b] is None else parts[b] + term
            after = after + logs[yy]
            near = near + logs[yy] * before[yy]
        agg.append(whole)
        totals.append(after)
        for b in range(ybits):
            shi[slots[zz], b * P_SIZE : (b + 1) * P_SIZE, :] = parts[b].astype(BF16)
    starts = [jnp.zeros((1, N), F32)]
    for zz in range(nz):
        starts.append(starts[-1] + totals[zz])
    block_logs = list(totals)
    for b in range(zbits):
        rows = slice((ybits + b) * P_SIZE, (ybits + b + 1) * P_SIZE)
        for zz in range(nz):
            if (zz >> b) & 1:
                scale = jnp.exp2(starts[zz] - starts[(zz >> b) << b] + lead[zz])
                shi[slots[zz], rows, :] = (agg[(zz >> b) - 1] * scale).astype(BF16)
            else:
                shi[slots[zz], rows, :] = jnp.zeros((P_SIZE, N), BF16)
        pairs = range(len(agg) // 2)
        agg = [jnp.exp2(block_logs[2 * m + 1]) * agg[2 * m] + agg[2 * m + 1] for m in pairs]
        block_logs = [block_logs[2 * m] + block_logs[2 * m + 1] for m in pairs]


def span_mix(k, r, bb, cb, tiles, mix, slot):
    half = Q // 2
    tri = lax.broadcasted_iota(jnp.int32, (half, half), 0) <= lax.broadcasted_iota(
        jnp.int32, (half, half), 1
    )
    at = span_at(k)
    b = bb[r, at, :]
    c = cb[r, at, :]
    tile = tiles[r, k]
    cum = tile[0:1, :]
    cum_col = jnp.transpose(tile)[:, 0:1]
    top = dot_nt(b[:half], c) * jnp.exp2(cum - cum_col[:half])
    low = dot_nt(b[half:], c[half:]) * jnp.exp2(cum[:, half:] - cum_col[half:])
    mix[slot, :half, :half] = jnp.where(tri, top[:, :half], 0.0).astype(BF16)
    mix[slot, :half, half:] = top[:, half:].astype(BF16)
    mix[slot, half:, half:] = jnp.where(tri, low, 0.0).astype(BF16)


def span_out(lev, k, low, r, skip, xb, cb, gb, slow, tiles, shi, ob, mix, slot):
    hi = lev - 1 - LO
    at = span_at(k)
    x = xb[r, :, at].astype(F32)
    c = cb[r, at, :]
    tile = tiles[r, k]
    cum = tile[0:1, :]
    xs = (x * tile[1:2, :]).astype(BF16)
    lw = gb[r, :, at].astype(F32)
    acc = dot(xs, mix[slot]) * lw[0:1] + skip * x
    bits = [bit for bit in range(LO) if bit >= STATIC or (low >> bit) & 1]
    parts = [slow[r, k, bit * P_SIZE : (bit + 1) * P_SIZE, :] for bit in bits] + [shi[r]]
    terms = dot_nt(jnp.concatenate(parts, axis=0), c)
    e_lo = jnp.exp2(cum)
    e_hi = jnp.exp2(cum + tile[2:3, :])
    rows = [(1 + bit, e_lo) for bit in bits] + [(1 + LO + bit, e_hi) for bit in range(hi)]
    for n, (row, e) in enumerate(rows):
        acc = acc + terms[n * P_SIZE : (n + 1) * P_SIZE] * (lw[row : row + 1] * e)
    ob[r, :, at] = acc.astype(BF16)


def shard_outputs(lev, r, first, count, skip, xb, bb, cb, gb, slow, tiles, shi, ob, mix):
    span_mix(first, r, bb, cb, tiles, mix, 0)
    group = 1 << STATIC

    def some(m, carry):
        base = first + group * m
        for low in range(group):
            k = base + low
            span_out(lev, k, low, r, skip, xb, cb, gb, slow, tiles, shi, ob, mix, low % 2)
            after = k + 1
            if low == group - 1:
                if count == group:
                    continue
                after = jnp.minimum(after, first + count - 1)
            span_mix(after, r, bb, cb, tiles, mix, (low + 1) % 2)
        return carry

    if count == group:
        some(0, 0)
    else:
        lax.fori_loop(0, count // group, some, 0)


def kernel(
    lev, sizes,
    x_ref, b_ref, c_ref, lg_ref, st_ref, lw_ref, skip_ref, out_ref,
    xb, bb, cb, gb, slow, tiles, sums, shi, ob, g_scr, st_scr, tmp, pk, mix, lwb, rowb,
    l_own, l_o, sent, r_x, r_g, r_z, r_h, r_n, r_f, r_s, r_m, r_o,
):
    nz, ny, nx, nc = sizes
    z, y, x, core = (lax.axis_index(a) for a in AXES)
    unit = SHARD // (nx * nc)
    rows = P_SIZE // ny
    other = 1 - core

    def turn(v, n):
        return lax.rem(v + n, n)

    def dev(dz=0, dy=0, dx=0, dc=0):
        return (turn(z + dz, nz), turn(y + dy, ny), turn(x + dx, nx), lax.rem(core + dc, nc))

    def rc(src, dst, send, recv, where):
        return pltpu.make_async_remote_copy(
            src_ref=src, dst_ref=dst, send_sem=send, recv_sem=recv,
            device_id=where, device_id_type=MESH,
        )

    def rel(i):
        odd = lax.rem(i, 2)
        return odd * ((i + 1) // 2) + (1 - odd) * lax.rem(nz - i // 2, nz)

    def cols(r, yy):
        at = (turn(z + r, nz) * ny + yy) * SHARD
        return pl.ds(pl.multiple_of(at, SHARD), SHARD)

    def band(yy):
        return pl.ds(pl.multiple_of(yy * rows, rows), rows)

    peers = [dev(dz=d) for d in range(1, nz)] + [dev(dy=d) for d in range(1, ny)]
    if nx > 1:
        peers += [dev(dx=1), dev(dx=-1)]
    if nc > 1:
        peers += [dev(dc=1)]
    barrier = pltpu.get_barrier_semaphore()
    for where in peers:
        pl.semaphore_signal(barrier, inc=1, device_id=where, device_id_type=MESH)

    src = (b_ref, c_ref)
    buf = (bb, cb)

    def piece(q, r, xx, cc, part=None):
        at = (xx * nc + cc) * unit
        size = unit
        if part is not None:
            size = unit // 2
            at = at + part * size
        return buf[q].at[r, pl.ds(pl.multiple_of(at, size), size), :]

    def own_copy(q):
        return pltpu.make_async_copy(src[q], piece(q, 0, x, core), l_own.at[q])

    def x_local(r):
        return pltpu.make_async_copy(x_ref.at[:, cols(r, y)], xb.at[r, band(y), :], r_x.at[r])

    def x_send(r, d):
        to = turn(y + d, ny)
        return rc(
            x_ref.at[:, cols(r, to)], xb.at[r, band(y), :], sent.at[0], r_x.at[r], dev(dy=d)
        )

    def bulk(ref, send, recv):
        return rc(ref, ref, send, recv, peers[0])

    def some(q, count):
        if count % SHARD == 0:
            return buf[q].at[pl.ds(0, count // SHARD)]
        return buf[q].at[0, pl.ds(0, count), :]

    mid = nz // 2

    def z_send(q, r, side, part=None):
        to = lax.rem(r - 1 + nz, nz) if side == 0 else r + 1
        arrived = r_z.at[q, to] if part is None or side == 0 else r_h.at[q]
        return rc(
            piece(q, r, x, core, part), piece(q, to, x, core, part),
            sent.at[4 + q], arrived, dev(dz=1 - 2 * side),
        )

    def z_each(q, r, act):
        ahead = lax.rem(nz - r, nz)

        @pl.when(((r == 0) | (r > mid)) & (ahead + 1 < mid))
        def _():
            act(z_send(q, r, 0))

        @pl.when(((r == 0) | (r > mid)) & (ahead + 1 == mid))
        def _():
            act(z_send(q, r, 0, 0))

        @pl.when(r + 1 < mid)
        def _():
            act(z_send(q, r, 1))

        @pl.when(r + 1 == mid)
        def _():
            act(z_send(q, r, 1, 1))

    def z_wait(q, r):
        @pl.when(r != mid)
        def _():
            ref = piece(q, r, x, core)
            rc(ref, ref, sent.at[4 + q], r_z.at[q, r], dev(dz=1)).wait_recv()

        @pl.when(r == mid)
        def _():
            ref = piece(q, r, x, core, 0)
            rc(ref, ref, sent.at[4 + q], r_z.at[q, r], dev(dz=1)).wait_recv()
            ref = piece(q, r, x, core, 1)
            rc(ref, ref, sent.at[4 + q], r_h.at[q], dev(dz=-1)).wait_recv()

    def g_send(r):
        o = nz - r
        return rc(pk.at[turn(z + o, nz)], gb.at[r], sent.at[1], r_g.at[r], dev(dz=o))

    def n_send(q, r, side, origin):
        part = piece(q, r, origin, core)
        return rc(part, part, sent.at[6 + q], r_n.at[q, r], dev(dx=1 - 2 * side))

    def f_send(q, r, side, origin):
        part = piece(q, r, origin, core, side)
        return rc(part, part, sent.at[8 + q], r_f.at[q, r], dev(dx=1 - 2 * side))

    def s_send(q, r, kind, cc):
        xx, part = ((0, None), (-1, None), (1, None), (-2, 0), (2, 1))[kind]
        ref = piece(q, r, turn(x + xx, nx), cc, part)
        return rc(ref, ref, sent.at[10 + q], r_s.at[q, r], dev(dc=1))

    kinds = 5 if nx > 1 else 1

    def step_a(q, i):
        r = rel(i)

        @pl.when(i == 0)
        def _():
            own_copy(q).wait()

        @pl.when(i > 0)
        def _():
            z_wait(q, r)

        z_each(q, r, lambda copy: copy.start())

        if nx > 1:
            n_send(q, r, 0, x).start()
            n_send(q, r, 1, x).start()
        if nc > 1:
            s_send(q, r, 0, core).start()

    def step_b(q, i):
        if nx > 1:
            r = rel(i)
            bulk(some(q, 2 * unit), sent.at[6 + q], r_n.at[q, r]).wait_recv()
            for side, origin in ((0, turn(x - 1, nx)), (1, turn(x + 1, nx))):
                f_send(q, r, side, origin).start()
                if nc > 1:
                    s_send(q, r, 1 + side, core).start()

    def step_c(q, i):
        if nx > 1:
            r = rel(i)
            bulk(some(q, unit), sent.at[8 + q], r_f.at[q, r]).wait_recv()
            if nc > 1:
                for kind in (3, 4):
                    s_send(q, r, kind, core).start()

    def step_s(q, i):
        if nc > 1:
            r = rel(i)
            bulk(some(q, nx * unit), sent.at[10 + q], r_s.at[q, r]).wait_recv()

    def m_send(r, d):
        ref = sums.at[y, r]
        return rc(ref, ref, sent.at[2], r_m.at[0], dev(dy=d))

    part_size = SHARD // 2

    def out_cols(r, part, yy):
        at = (turn(z + r, nz) * ny + yy) * SHARD + part * part_size
        return pl.ds(pl.multiple_of(at, part_size), part_size)

    def here(part):
        return pl.ds(pl.multiple_of(part * part_size, part_size), part_size)

    def o_send(r, part, d):
        to = turn(y + d, ny)
        return rc(
            ob.at[r, band(to), here(part)], out_ref.at[:, out_cols(r, part, y)],
            sent.at[3], r_o.at[0], dev(dy=d),
        )

    def o_local(r, part):
        return pltpu.make_async_copy(
            ob.at[r, band(y), here(part)], out_ref.at[:, out_cols(r, part, y)], l_o.at[0]
        )

    loads = [
        pltpu.make_async_copy(lw_ref, lwb, l_own.at[2]),
        pltpu.make_async_copy(lg_ref, rowb.at[0], l_own.at[3]),
        pltpu.make_async_copy(st_ref, rowb.at[1], l_own.at[4]),
    ]
    own_copy(0).start()
    own_copy(1).start()
    for copy in loads:
        copy.start()
    mix[...] = jnp.zeros_like(mix)
    pl.semaphore_wait(barrier, len(peers))

    def begin(i, carry):
        r = rel(i)
        x_local(r).start()
        for d in range(1, ny):
            x_send(r, d).start()
        return carry

    lax.fori_loop(0, nz, begin, 0)
    step_a(0, 0)
    for copy in loads:
        copy.wait()
    pack_gates(lev, z, lwb, rowb.at[0], rowb.at[1], tmp, pk)
    gb[0] = pk[z]

    def inward(i, carry):
        @pl.when((i >= 1) & (i < nz))
        def _():
            step_a(0, i)

        @pl.when((i >= 1) & (i <= nz))
        def _():
            step_b(0, i - 1)

        @pl.when((i >= 2) & (i <= nz + 1))
        def _():
            step_c(0, i - 2)

        @pl.when((i >= 1) & (i < nz))
        def _():
            r = rel(i)
            pack_gates(lev, turn(z - r, nz), lwb, rowb.at[0], rowb.at[1], tmp, pk)
            g_send(r).start()

        @pl.when((i >= nz) & (i < 2 * nz))
        def _():
            step_a(1, i - nz)

        @pl.when(i >= nz + 1)
        def _():
            step_b(1, i - nz - 1)

        @pl.when(i >= nz + 2)
        def _():
            step_c(1, i - nz - 2)

        @pl.when(i >= 3)
        def _():
            r = rel(i - 3)
            step_s(0, i - 3)

            @pl.when(i > 3)
            def _():
                g_send(r).wait_recv()

            bulk(xb.at[r], sent.at[0], r_x.at[r]).wait_recv()
            state, log = shard_states(lev, r, xb, bb, gb, slow, tiles, g_scr, st_scr)
            sums[y, r, 0:P_SIZE, :] = state.astype(BF16)
            first = log.astype(BF16).astype(F32)
            rest = log - first
            second = rest.astype(BF16).astype(F32)
            logs = jnp.concatenate([first, second, rest - second, jnp.zeros((13, N), F32)], axis=0)
            sums[y, r, P_SIZE : P_SIZE + 16, :] = logs.astype(BF16)
            for d in range(1, ny):
                m_send(r, d).start()

        return carry

    lax.fori_loop(1, nz + 3, inward, 0)

    bulk(sums.at[pl.ds(0, ny - 1)], sent.at[2], r_m.at[0]).wait_recv()
    shard_levels(nz, ny, z, y, sums, shi)
    skip = skip_ref[z]
    early = min(3, nz)

    def outward(j, carry):
        i, part = j // 2, lax.rem(j, 2)
        r = rel(i)

        @pl.when(part == 0)
        def _():
            @pl.when(i + early < nz)
            def _():
                step_a(1, i + early)

            @pl.when(i + 2 < nz)
            def _():
                step_b(1, i + 2)

            @pl.when(i + 1 < nz)
            def _():
                step_c(1, i + 1)

            step_s(1, i)

        half = SPANS // 2
        shard_outputs(
            lev, r, part * half, half, skip, xb, bb, cb, gb, slow, tiles, shi, ob, mix
        )
        o_local(r, part).start()
        for d in range(1, ny):
            o_send(r, part, d).start()
        return carry

    lax.fori_loop(0, 2 * nz, outward, 0)

    away = nz * (ny - 1) * rows * SHARD // (P_SIZE * SHARD)
    bulk(xb.at[pl.ds(0, away)], sent.at[0], r_x.at[0]).wait_send()
    bulk(pk.at[pl.ds(0, nz - 1)], sent.at[1], r_g.at[0]).wait_send()
    bulk(sums.at[pl.ds(0, ny - 1)], sent.at[2], r_m.at[0]).wait_send()
    bulk(ob.at[pl.ds(0, away)], sent.at[3], r_o.at[0]).wait_send()
    for q in range(2):
        bulk(some(q, (nz - 1) * unit), sent.at[4 + q], r_h.at[q]).wait_send()
        if nx > 1:
            bulk(some(q, 2 * nz * unit), sent.at[6 + q], r_h.at[q]).wait_send()
            bulk(some(q, nz * unit), sent.at[8 + q], r_h.at[q]).wait_send()
        if nc > 1:
            bulk(some(q, nx * nz * unit), sent.at[10 + q], r_h.at[q]).wait_send()
    bulk(ob.at[pl.ds(0, away)], sent.at[3], r_o.at[0]).wait_recv()
    mine = ob.at[pl.ds(0, nz // ny)]
    pltpu.make_async_copy(mine, mine, l_o.at[0]).wait()


def on_device(x_heads, b_proj, c_proj, log_gate, step_size, level_weight, skip):
    nz, ny, nx, nc = sizes = tuple(lax.axis_size(a) for a in AXES)
    lev = level_weight.shape[1]
    hi = lev - 1 - LO
    rows, tok = x_heads.shape
    any_spec = pl.BlockSpec(memory_space=pl.ANY)
    dma = lambda *shape: pltpu.SemaphoreType.DMA(shape)
    return pl.pallas_call(
        functools.partial(kernel, lev, sizes),
        out_shape=pltpu.VMEM((rows, tok), BF16),
        in_specs=[any_spec, any_spec, any_spec, any_spec, any_spec, any_spec,
                  pl.BlockSpec(memory_space=pltpu.SMEM)],
        out_specs=any_spec,
        scratch_shapes=[
            pltpu.VMEM((nz, P_SIZE, SHARD), BF16),
            pltpu.VMEM((nz, SHARD, N), BF16),
            pltpu.VMEM((nz, SHARD, N), BF16),
            pltpu.VMEM((nz, 16, SHARD), BF16),
            pltpu.VMEM((nz, SPANS, LO * P_SIZE, N), BF16),
            pltpu.VMEM((nz, SPANS, 8, Q), F32),
            pltpu.VMEM((ny, nz, P_SIZE + 16, N), BF16),
            pltpu.VMEM((nz, hi * P_SIZE, N), BF16),
            pltpu.VMEM((nz, P_SIZE, SHARD), BF16),
            pltpu.VMEM((4, SPANS, Q), F32),
            pltpu.VMEM((SPANS, P_SIZE, N), F32),
            pltpu.VMEM((16, SHARD), F32),
            pltpu.VMEM((nz, 16, SHARD), BF16),
            pltpu.VMEM((2, Q, Q), BF16),
            pltpu.VMEM((lev, nz, SHARD), F32),
            pltpu.VMEM((2, nz, SHARD), F32),
            dma(5), dma(1), dma(12),
            dma(nz), dma(nz), dma(2, nz), dma(2), dma(2, nz), dma(2, nz), dma(2, nz), dma(1), dma(1),
        ],
        compiler_params=pltpu.CompilerParams(
            collective_id=0, has_side_effects=True, vmem_limit_bytes=56 << 20
        ),
        name="layer",
    )(x_heads, b_proj, c_proj, log_gate, step_size, jnp.swapaxes(level_weight, 0, 1), skip)


def build(mesh):
    group = ("x", "core")
    seq = ("z", "y")
    in_specs = (
        P(group + seq, None),
        P(seq + group, None),
        P(seq + group, None),
        P(group, seq),
        P(group, seq),
        P(group, None, seq),
        P(group),
    )
    return jax.shard_map(
        on_device, mesh=mesh, in_specs=in_specs, out_specs=P(group + seq, None), check_vma=False
    )


def solution(mesh):
    return build(Mesh(mesh.devices.reshape(8, 4, 4, 2), AXES))
```

```python
import functools

import jax
import jax.numpy as jnp
from jax import lax
from jax.experimental import pallas as pl
from jax.experimental.pallas import tpu as pltpu
from jax.sharding import Mesh, PartitionSpec as P

P_SIZE = 64
N = 128
Q = 256
LO = 4
SPANS = 1 << LO
STATIC = 2
GROUP = 1 << STATIC
SHARD = SPANS * Q
LOG2E = 1.4426950408889634
NT = (((1,), (1,)), ((), ()))
F32 = jnp.float32
BF16 = jnp.bfloat16
MESH = pl.DeviceIdType.MESH
AXES = ("z", "y", "x", "core")


def dot(a, b):
    return jnp.dot(a, b, preferred_element_type=F32)


def dot_nt(a, b):
    return lax.dot_general(a, b, NT, preferred_element_type=F32)


def span_at(k):
    return pl.ds(pl.multiple_of(k * Q, Q), Q)


def pack_gates(lev, h, lw_ref, lg_ref, st_ref, tmp, pk):
    for row in range(lev):
        tmp[row : row + 1, :] = lw_ref[row, pl.ds(h, 1), :]
    for row, ref in ((lev, lg_ref), (lev + 3, st_ref)):
        v = ref[pl.ds(h, 1), :]
        first = v.astype(BF16).astype(F32)
        rest = v - first
        second = rest.astype(BF16).astype(F32)
        tmp[row : row + 1, :] = first
        tmp[row + 1 : row + 2, :] = second
        tmp[row + 2 : row + 3, :] = rest - second
    pk[h] = tmp[...].astype(BF16)


def shard_states(lev, r, arrive, xb, bb, gb, slow, tiles, g_scr, st_scr):
    for k in range(SPANS):
        piece = gb[r, :, k * Q : (k + 1) * Q].astype(F32)
        for m in range(3):
            g_scr[m, k : k + 1, :] = piece[lev + m : lev + m + 1]
        g_scr[3, k : k + 1, :] = (
            piece[lev + 3 : lev + 4] + piece[lev + 4 : lev + 5] + piece[lev + 5 : lev + 6]
        )
    upper = (
        lax.broadcasted_iota(jnp.int32, (Q, Q), 0) <= lax.broadcasted_iota(jnp.int32, (Q, Q), 1)
    ).astype(BF16)
    cum = dot(g_scr[0].astype(BF16), upper)
    cum = cum + dot(g_scr[1].astype(BF16), upper)
    cum = (cum + dot(g_scr[2].astype(BF16), upper)) * LOG2E
    step = g_scr[3]
    g_scr[0] = jnp.exp2(cum[:, Q - 1 :] - cum) * step
    logs = [jnp.broadcast_to(cum[k : k + 1, Q - 1 :], (1, N)) for k in range(SPANS)]
    starts = [jnp.zeros((1, N), F32)]
    for k in range(SPANS):
        starts.append(starts[-1] + logs[k])
    for k in range(SPANS):
        tiles[r, k, 0:1, :] = cum[k : k + 1]
        tiles[r, k, 1:2, :] = step[k : k + 1]
        tiles[r, k, 2:3, :] = jnp.concatenate([starts[k], starts[k]], axis=1)

    arrive()

    def one(k, carry):
        w = xb[r, :, span_at(k)].astype(F32) * g_scr[0, pl.ds(k, 1), :]
        st_scr[k] = dot(w.astype(BF16), bb[r, span_at(k), :])
        return carry

    lax.fori_loop(0, SPANS, one, 0, unroll=2)
    agg = [st_scr[k] for k in range(SPANS)]
    block_logs = list(logs)
    for bit in range(LO):
        rows = slice(bit * P_SIZE, (bit + 1) * P_SIZE)
        for k in range(SPANS):
            if (k >> bit) & 1:
                scale = jnp.exp2(starts[k] - starts[(k >> bit) << bit])
                slow[r, k, rows, :] = (agg[(k >> bit) - 1] * scale).astype(BF16)
            else:
                slow[r, k, rows, :] = jnp.zeros((P_SIZE, N), BF16)
        pairs = range(len(agg) // 2)
        agg = [jnp.exp2(block_logs[2 * m + 1]) * agg[2 * m] + agg[2 * m + 1] for m in pairs]
        block_logs = [block_logs[2 * m] + block_logs[2 * m + 1] for m in pairs]
    return agg[0], block_logs[0]


def shard_levels(nz, ny, z, y, sums, shi):
    ybits = ny.bit_length() - 1
    zbits = nz.bit_length() - 1
    slots = [lax.rem(zz - z + nz, nz) for zz in range(nz)]
    before = [jnp.where(yy < y, 1.0, 0.0) for yy in range(ny)]
    belongs = []
    for b in range(ybits):
        own = y // (1 << b)
        odd = lax.rem(own, 2) == 1
        belongs.append(
            [jnp.where(odd & (own - 1 == yy >> b), 1.0, 0.0) for yy in range(ny)]
        )
    agg, totals, lead = [], [], []
    for zz in range(nz):
        logs = []
        for yy in range(ny):
            block = sums[yy, slots[zz], P_SIZE : P_SIZE + 16, :].astype(F32)
            logs.append(block[0:1] + block[1:2] + block[2:3])
        ahead = logs[0] * before[0]
        for yy in range(1, ny):
            ahead = ahead + logs[yy] * before[yy]
        lead.append(ahead)
        after = jnp.zeros((1, N), F32)
        near = jnp.zeros((1, N), F32)
        whole = None
        parts = [None] * ybits
        for yy in reversed(range(ny)):
            state = sums[yy, slots[zz], 0:P_SIZE, :].astype(F32)
            term = state * jnp.exp2(after)
            whole = term if whole is None else whole + term
            scale = jnp.exp2(near)
            for b in range(ybits):
                term = state * (scale * belongs[b][yy])
                parts[b] = term if parts[b] is None else parts[b] + term
            after = after + logs[yy]
            near = near + logs[yy] * before[yy]
        agg.append(whole)
        totals.append(after)
        for b in range(ybits):
            shi[slots[zz], b * P_SIZE : (b + 1) * P_SIZE, :] = parts[b].astype(BF16)
    starts = [jnp.zeros((1, N), F32)]
    for zz in range(nz):
        starts.append(starts[-1] + totals[zz])
    block_logs = list(totals)
    for b in range(zbits):
        rows = slice((ybits + b) * P_SIZE, (ybits + b + 1) * P_SIZE)
        for zz in range(nz):
            if (zz >> b) & 1:
                scale = jnp.exp2(starts[zz] - starts[(zz >> b) << b] + lead[zz])
                shi[slots[zz], rows, :] = (agg[(zz >> b) - 1] * scale).astype(BF16)
            else:
                shi[slots[zz], rows, :] = jnp.zeros((P_SIZE, N), BF16)
        pairs = range(len(agg) // 2)
        agg = [jnp.exp2(block_logs[2 * m + 1]) * agg[2 * m] + agg[2 * m + 1] for m in pairs]
        block_logs = [block_logs[2 * m] + block_logs[2 * m + 1] for m in pairs]


def span_mix(k, r, bb, cb, tiles, mix, slot):
    half = Q // 2
    tri = lax.broadcasted_iota(jnp.int32, (half, half), 0) <= lax.broadcasted_iota(
        jnp.int32, (half, half), 1
    )
    at = span_at(k)
    b = bb[r, at, :]
    c = cb[r, at, :]
    tile = tiles[r, k]
    cum = tile[0:1, :]
    cum_col = jnp.transpose(tile)[:, 0:1]
    top = dot_nt(b[:half], c) * jnp.exp2(cum - cum_col[:half])
    low = dot_nt(b[half:], c[half:]) * jnp.exp2(cum[:, half:] - cum_col[half:])
    mix[slot, :half, :half] = jnp.where(tri, top[:, :half], 0.0).astype(BF16)
    mix[slot, :half, half:] = top[:, half:].astype(BF16)
    mix[slot, half:, half:] = jnp.where(tri, low, 0.0).astype(BF16)


def span_out(lev, k, low, r, skip, xb, cb, gb, slow, tiles, shi, ob, mix, slot):
    hi = lev - 1 - LO
    at = span_at(k)
    x = xb[r, :, at].astype(F32)
    c = cb[r, at, :]
    tile = tiles[r, k]
    cum = tile[0:1, :]
    xs = (x * tile[1:2, :]).astype(BF16)
    lw = gb[r, :, at].astype(F32)
    acc = dot(xs, mix[slot]) * lw[0:1] + skip * x
    bits = [bit for bit in range(LO) if bit >= STATIC or (low >> bit) & 1]
    parts = [slow[r, k, bit * P_SIZE : (bit + 1) * P_SIZE, :] for bit in bits] + [shi[r]]
    terms = dot_nt(jnp.concatenate(parts, axis=0), c)
    e_lo = jnp.exp2(cum)
    e_hi = jnp.exp2(cum + tile[2:3, :])
    rows = [(1 + bit, e_lo) for bit in bits] + [(1 + LO + bit, e_hi) for bit in range(hi)]
    for n, (row, e) in enumerate(rows):
        acc = acc + terms[n * P_SIZE : (n + 1) * P_SIZE] * (lw[row : row + 1] * e)
    ob[r, :, at] = acc.astype(BF16)


def shard_outputs(lev, r, skip, flush, xb, bb, cb, gb, slow, tiles, shi, ob, mix):
    span_mix(0, r, bb, cb, tiles, mix, 0)

    def some(m, carry):
        for low in range(GROUP):
            k = GROUP * m + low
            span_out(lev, k, low, r, skip, xb, cb, gb, slow, tiles, shi, ob, mix, low % 2)
            span_mix(jnp.minimum(k + 1, SPANS - 1), r, bb, cb, tiles, mix, (low + 1) % 2)
        flush(m)
        return carry

    lax.fori_loop(0, SPANS // GROUP, some, 0)


def kernel(
    lev, sizes,
    x_ref, b_ref, c_ref, lg_ref, st_ref, lw_ref, skip_ref, out_ref,
    xb, bb, cb, gb, slow, tiles, sums, shi, ob, g_scr, st_scr, tmp, pk, mix, lwb, rowb,
    l_own, l_o, sent, r_x, r_g, r_z, r_h, r_n, r_f, r_s, r_m, r_o,
):
    nz, ny, nx, nc = sizes
    z, y, x, core = (lax.axis_index(a) for a in AXES)
    unit = SHARD // (nx * nc)
    rows = P_SIZE // ny
    other = 1 - core

    def turn(v, n):
        return lax.rem(v + n, n)

    def dev(dz=0, dy=0, dx=0, dc=0):
        return (turn(z + dz, nz), turn(y + dy, ny), turn(x + dx, nx), lax.rem(core + dc, nc))

    def rc(src, dst, send, recv, where):
        return pltpu.make_async_remote_copy(
            src_ref=src, dst_ref=dst, send_sem=send, recv_sem=recv,
            device_id=where, device_id_type=MESH,
        )

    def rel(i):
        odd = lax.rem(i, 2)
        return odd * ((i + 1) // 2) + (1 - odd) * lax.rem(nz - i // 2, nz)

    def cols(r, yy):
        at = (turn(z + r, nz) * ny + yy) * SHARD
        return pl.ds(pl.multiple_of(at, SHARD), SHARD)

    def band(yy):
        return pl.ds(pl.multiple_of(yy * rows, rows), rows)

    peers = [dev(dz=d) for d in range(1, nz)] + [dev(dy=d) for d in range(1, ny)]
    if nx > 1:
        peers += [dev(dx=1), dev(dx=-1)]
    if nc > 1:
        peers += [dev(dc=1)]
    barrier = pltpu.get_barrier_semaphore()
    for where in peers:
        pl.semaphore_signal(barrier, inc=1, device_id=where, device_id_type=MESH)

    src = (b_ref, c_ref)
    buf = (bb, cb)

    def piece(q, r, xx, cc, part=None):
        at = (xx * nc + cc) * unit
        size = unit
        if part is not None:
            size = unit // 2
            at = at + part * size
        return buf[q].at[r, pl.ds(pl.multiple_of(at, size), size), :]

    def own_copy(q):
        return pltpu.make_async_copy(src[q], piece(q, 0, x, core), l_own.at[q])

    def x_local(r):
        return pltpu.make_async_copy(x_ref.at[:, cols(r, y)], xb.at[r, band(y), :], r_x.at[r])

    def x_send(r, d):
        to = turn(y + d, ny)
        return rc(
            x_ref.at[:, cols(r, to)], xb.at[r, band(y), :], sent.at[0], r_x.at[r], dev(dy=d)
        )

    def bulk(ref, send, recv):
        return rc(ref, ref, send, recv, peers[0])

    def some(q, count):
        if count % SHARD == 0:
            return buf[q].at[pl.ds(0, count // SHARD)]
        return buf[q].at[0, pl.ds(0, count), :]

    mid = nz // 2

    def z_send(q, r, side, part=None):
        to = lax.rem(r - 1 + nz, nz) if side == 0 else r + 1
        arrived = r_z.at[q, to] if part is None or side == 0 else r_h.at[q]
        return rc(
            piece(q, r, x, core, part), piece(q, to, x, core, part),
            sent.at[4 + q], arrived, dev(dz=1 - 2 * side),
        )

    def z_each(q, r, act):
        ahead = lax.rem(nz - r, nz)

        @pl.when(((r == 0) | (r > mid)) & (ahead + 1 < mid))
        def _():
            act(z_send(q, r, 0))

        @pl.when(((r == 0) | (r > mid)) & (ahead + 1 == mid))
        def _():
            act(z_send(q, r, 0, 0))

        @pl.when(r + 1 < mid)
        def _():
            act(z_send(q, r, 1))

        @pl.when(r + 1 == mid)
        def _():
            act(z_send(q, r, 1, 1))

    def z_wait(q, r):
        @pl.when(r != mid)
        def _():
            ref = piece(q, r, x, core)
            rc(ref, ref, sent.at[4 + q], r_z.at[q, r], dev(dz=1)).wait_recv()

        @pl.when(r == mid)
        def _():
            ref = piece(q, r, x, core, 0)
            rc(ref, ref, sent.at[4 + q], r_z.at[q, r], dev(dz=1)).wait_recv()
            ref = piece(q, r, x, core, 1)
            rc(ref, ref, sent.at[4 + q], r_h.at[q], dev(dz=-1)).wait_recv()

    def g_send(r):
        o = nz - r
        return rc(pk.at[turn(z + o, nz)], gb.at[r], sent.at[1], r_g.at[r], dev(dz=o))

    def n_send(q, r, side, origin):
        part = piece(q, r, origin, core)
        return rc(part, part, sent.at[6 + q], r_n.at[q, r], dev(dx=1 - 2 * side))

    def f_send(q, r, side, origin):
        part = piece(q, r, origin, core, side)
        return rc(part, part, sent.at[8 + q], r_f.at[q, r], dev(dx=1 - 2 * side))

    def s_send(q, r, kind, cc):
        xx, part = ((0, None), (-1, None), (1, None), (-2, 0), (2, 1))[kind]
        ref = piece(q, r, turn(x + xx, nx), cc, part)
        return rc(ref, ref, sent.at[10 + q], r_s.at[q, r], dev(dc=1))

    kinds = 5 if nx > 1 else 1

    def step_a(q, i):
        r = rel(i)

        @pl.when(i == 0)
        def _():
            own_copy(q).wait()

        @pl.when(i > 0)
        def _():
            z_wait(q, r)

        z_each(q, r, lambda copy: copy.start())

        if nx > 1:
            n_send(q, r, 0, x).start()
            n_send(q, r, 1, x).start()
        if nc > 1:
            s_send(q, r, 0, core).start()

    def step_b(q, i):
        if nx > 1:
            r = rel(i)
            bulk(some(q, 2 * unit), sent.at[6 + q], r_n.at[q, r]).wait_recv()
            for side, origin in ((0, turn(x - 1, nx)), (1, turn(x + 1, nx))):
                f_send(q, r, side, origin).start()
                if nc > 1:
                    s_send(q, r, 1 + side, core).start()

    def step_c(q, i):
        if nx > 1:
            r = rel(i)
            bulk(some(q, unit), sent.at[8 + q], r_f.at[q, r]).wait_recv()
            if nc > 1:
                for kind in (3, 4):
                    s_send(q, r, kind, core).start()

    def step_s(q, i):
        if nc > 1:
            r = rel(i)
            bulk(some(q, nx * unit), sent.at[10 + q], r_s.at[q, r]).wait_recv()

    def m_send(r, d):
        ref = sums.at[y, r]
        return rc(ref, ref, sent.at[2], r_m.at[0], dev(dy=d))

    part_size = GROUP * Q

    def out_cols(r, part, yy):
        at = (turn(z + r, nz) * ny + yy) * SHARD + part * part_size
        return pl.ds(pl.multiple_of(at, part_size), part_size)

    def here(part):
        return pl.ds(pl.multiple_of(part * part_size, part_size), part_size)

    def o_send(r, part, d):
        to = turn(y + d, ny)
        return rc(
            ob.at[r, band(to), here(part)], out_ref.at[:, out_cols(r, part, y)],
            sent.at[3], r_o.at[0], dev(dy=d),
        )

    def o_local(r, part):
        return pltpu.make_async_copy(
            ob.at[r, band(y), here(part)], out_ref.at[:, out_cols(r, part, y)], l_o.at[0]
        )

    loads = [
        pltpu.make_async_copy(lw_ref, lwb, l_own.at[2]),
        pltpu.make_async_copy(lg_ref, rowb.at[0], l_own.at[3]),
        pltpu.make_async_copy(st_ref, rowb.at[1], l_own.at[4]),
    ]
    own_copy(0).start()
    own_copy(1).start()
    for copy in loads:
        copy.start()
    mix[...] = jnp.zeros_like(mix)
    pl.semaphore_wait(barrier, len(peers))

    def begin(i, carry):
        r = rel(i)
        x_local(r).start()
        for d in (2, 1, 3):
            if d < ny:
                x_send(r, d).start()
        return carry

    lax.fori_loop(0, nz, begin, 0)
    step_a(0, 0)
    for copy in loads:
        copy.wait()
    pack_gates(lev, z, lwb, rowb.at[0], rowb.at[1], tmp, pk)
    gb[0] = pk[z]

    def inward(i, carry):
        @pl.when((i >= 1) & (i < nz))
        def _():
            step_a(0, i)

        @pl.when((i >= 1) & (i <= nz))
        def _():
            step_b(0, i - 1)

        @pl.when((i >= 2) & (i <= nz + 1))
        def _():
            step_c(0, i - 2)

        @pl.when((i >= 1) & (i < nz))
        def _():
            r = rel(i)
            pack_gates(lev, turn(z - r, nz), lwb, rowb.at[0], rowb.at[1], tmp, pk)
            g_send(r).start()

        @pl.when((i >= nz) & (i < 2 * nz))
        def _():
            step_a(1, i - nz)

        @pl.when(i >= nz + 1)
        def _():
            step_b(1, i - nz - 1)

        @pl.when(i >= nz + 2)
        def _():
            step_c(1, i - nz - 2)

        @pl.when(i >= 3)
        def _():
            r = rel(i - 3)
            step_s(0, i - 3)

            @pl.when(i > 3)
            def _():
                g_send(r).wait_recv()

            arrive = bulk(xb.at[r], sent.at[0], r_x.at[r]).wait_recv
            state, log = shard_states(lev, r, arrive, xb, bb, gb, slow, tiles, g_scr, st_scr)
            sums[y, r, 0:P_SIZE, :] = state.astype(BF16)
            first = log.astype(BF16).astype(F32)
            rest = log - first
            second = rest.astype(BF16).astype(F32)
            logs = jnp.concatenate([first, second, rest - second, jnp.zeros((13, N), F32)], axis=0)
            sums[y, r, P_SIZE : P_SIZE + 16, :] = logs.astype(BF16)
            for d in range(1, ny):
                m_send(r, d).start()

        return carry

    lax.fori_loop(1, nz + 3, inward, 0)

    bulk(sums.at[pl.ds(0, ny - 1)], sent.at[2], r_m.at[0]).wait_recv()
    shard_levels(nz, ny, z, y, sums, shi)
    skip = skip_ref[z]
    early = min(3, nz)

    def outward(i, carry):
        r = rel(i)

        @pl.when(i + early < nz)
        def _():
            step_a(1, i + early)

        @pl.when(i + 2 < nz)
        def _():
            step_b(1, i + 2)

        @pl.when(i + 1 < nz)
        def _():
            step_c(1, i + 1)

        step_s(1, i)

        def flush(part):
            for d in (2, 1, 3):
                if d < ny:
                    o_send(r, part, d).start()
            o_local(r, part).start()

        shard_outputs(lev, r, skip, flush, xb, bb, cb, gb, slow, tiles, shi, ob, mix)
        return carry

    lax.fori_loop(0, nz, outward, 0)

    away = nz * (ny - 1) * rows * SHARD // (P_SIZE * SHARD)
    bulk(xb.at[pl.ds(0, away)], sent.at[0], r_x.at[0]).wait_send()
    bulk(pk.at[pl.ds(0, nz - 1)], sent.at[1], r_g.at[0]).wait_send()
    bulk(sums.at[pl.ds(0, ny - 1)], sent.at[2], r_m.at[0]).wait_send()
    bulk(ob.at[pl.ds(0, away)], sent.at[3], r_o.at[0]).wait_send()
    for q in range(2):
        bulk(some(q, (nz - 1) * unit), sent.at[4 + q], r_h.at[q]).wait_send()
        if nx > 1:
            bulk(some(q, 2 * nz * unit), sent.at[6 + q], r_h.at[q]).wait_send()
            bulk(some(q, nz * unit), sent.at[8 + q], r_h.at[q]).wait_send()
        if nc > 1:
            bulk(some(q, nx * nz * unit), sent.at[10 + q], r_h.at[q]).wait_send()
    bulk(ob.at[pl.ds(0, away)], sent.at[3], r_o.at[0]).wait_recv()
    mine = ob.at[pl.ds(0, nz // ny)]
    pltpu.make_async_copy(mine, mine, l_o.at[0]).wait()


def on_device(x_heads, b_proj, c_proj, log_gate, step_size, level_weight, skip):
    nz, ny, nx, nc = sizes = tuple(lax.axis_size(a) for a in AXES)
    lev = level_weight.shape[1]
    hi = lev - 1 - LO
    rows, tok = x_heads.shape
    any_spec = pl.BlockSpec(memory_space=pl.ANY)
    dma = lambda *shape: pltpu.SemaphoreType.DMA(shape)
    return pl.pallas_call(
        functools.partial(kernel, lev, sizes),
        out_shape=pltpu.VMEM((rows, tok), BF16),
        in_specs=[any_spec, any_spec, any_spec, any_spec, any_spec, any_spec,
                  pl.BlockSpec(memory_space=pltpu.SMEM)],
        out_specs=any_spec,
        scratch_shapes=[
            pltpu.VMEM((nz, P_SIZE, SHARD), BF16),
            pltpu.VMEM((nz, SHARD, N), BF16),
            pltpu.VMEM((nz, SHARD, N), BF16),
            pltpu.VMEM((nz, 16, SHARD), BF16),
            pltpu.VMEM((nz, SPANS, LO * P_SIZE, N), BF16),
            pltpu.VMEM((nz, SPANS, 8, Q), F32),
            pltpu.VMEM((ny, nz, P_SIZE + 16, N), BF16),
            pltpu.VMEM((nz, hi * P_SIZE, N), BF16),
            pltpu.VMEM((nz, P_SIZE, SHARD), BF16),
            pltpu.VMEM((4, SPANS, Q), F32),
            pltpu.VMEM((SPANS, P_SIZE, N), F32),
            pltpu.VMEM((16, SHARD), F32),
            pltpu.VMEM((nz, 16, SHARD), BF16),
            pltpu.VMEM((2, Q, Q), BF16),
            pltpu.VMEM((lev, nz, SHARD), F32),
            pltpu.VMEM((2, nz, SHARD), F32),
            dma(5), dma(1), dma(12),
            dma(nz), dma(nz), dma(2, nz), dma(2), dma(2, nz), dma(2, nz), dma(2, nz), dma(1), dma(1),
        ],
        compiler_params=pltpu.CompilerParams(
            collective_id=0, has_side_effects=True, vmem_limit_bytes=56 << 20
        ),
        name="layer",
    )(x_heads, b_proj, c_proj, log_gate, step_size, jnp.swapaxes(level_weight, 0, 1), skip)


def build(mesh):
    group = ("x", "core")
    seq = ("z", "y")
    in_specs = (
        P(group + seq, None),
        P(seq + group, None),
        P(seq + group, None),
        P(group, seq),
        P(group, seq),
        P(group, None, seq),
        P(group),
    )
    return jax.shard_map(
        on_device, mesh=mesh, in_specs=in_specs, out_specs=P(group + seq, None), check_vma=False
    )


def solution(mesh):
    return build(Mesh(mesh.devices.reshape(8, 4, 4, 2), AXES))
```
